32 devices in a mesh: maps: 2 (over x), row: 4 (over y, core), col: 4 (over z).
Axes of the slice: x: 2, y: 2, z: 4, core: 2. Of those that a mesh axis runs over, the one named last changes fastest.
Arguments:
- shear: float32 [2, 2, 2048, 2048], P(None, 'maps', 'row', 'col'), parts along dimension 1, may hold values from -600 to 600
- smoothing: float32 [2], P('maps'), parts along dimension 0, may hold values from 0.6 to 1.2
- offsets: int32 [2, 128, 128], P('maps', ('row', 'col')), parts along dimension 0, may hold values from 0 to 255
- thresholds: int32 [2, 16], P('maps'), parts along dimension 0, may hold values from -4 to 19
Outputs:
- snr: float32 [2, 2048, 2048], P('maps', ('row', 'col')), parts along dimension 0
- heights: float32 [2, 128, 128], P('maps', ('row', 'col')), parts along dimension 0
- counts: float32 [2, 16], P('maps'), parts along dimension 0
The draws below stay inside these ranges and needn't reach their ends.
There are 2 independent parts, one for each index of `maps`. The reference program is written for one: setup_inputs(seed, part) draws one part's arguments, and reference() takes and returns one part's arrays. A program takes and returns all parts, laid end to end along the dimension named above; each array names one. Nothing has to cross between parts.
All inputs are finite; a program needn't handle non-finite values.
Results may differ from the reference program's by a relative error of at most 0.00014.
Values sent between devices are 32-bit elements; how exact they have to be, the bound alone decides.
A program may use at most 64 MiB of HBM per device.

```python
import math
import jax
import jax.numpy as jnp
from jax import lax

NX = 2048
NY = 2048
MAPS = 1
CELL = 16
NBINS = 16


def draw_shear(key, part):
    noise_key = jax.random.fold_in(jax.random.fold_in(key, 7), 0)
    ramp = 1.0 + 2.0 * jnp.arange(NX, dtype=jnp.float32) / (NX - 1)
    base = jnp.clip(jax.random.normal(noise_key, (2, MAPS, NX, NY), jnp.float32), -6.0, 6.0)
    return base * ramp[:, None]


def set_ends(drawn, rng, least, high):
    dims = drawn.shape
    spot = [jax.random.randint(jax.random.fold_in(rng, axis), (), 0, dims[axis]) for axis in range(len(dims))]
    drawn = drawn.at[tuple(spot)].set(least)
    longest = dims.index(max(dims))
    spot[longest] = (spot[longest] + 1) % dims[longest]
    return drawn.at[tuple(spot)].set(high)


def setup_inputs(seed: int = 0, part: int = 0) -> dict:
    splits = jax.random.split(jax.random.key(seed), 5)
    own_keys = jax.random.split(jax.random.fold_in(splits[4], part), 5)
    shear = draw_shear(jax.random.fold_in(jax.random.fold_in(splits[4], part), 71), part)
    smoothing = jnp.clip(jnp.exp(jax.random.uniform(own_keys[1], (MAPS,), jnp.float32, math.log(0.6), math.log(1.2))), 0.6, 1.2)
    offsets = set_ends(jax.random.randint(own_keys[2], (MAPS, NX // CELL, NY // CELL), 0, CELL * CELL), jax.random.fold_in(own_keys[2], 1), 0, (CELL * CELL) - 1).astype(jnp.int32)
    thresholds = set_ends(jax.random.randint(own_keys[3], (MAPS, NBINS), -4, 20), jax.random.fold_in(own_keys[3], 1), -4, 19).astype(jnp.int32)
    return dict(shear=shear, smoothing=smoothing, offsets=offsets, thresholds=thresholds)


def neighbour_max(field):
    nearest = None
    for step_row in (-1, 0, 1):
        for step_col in (-1, 0, 1):
            if step_row == 0 and step_col == 0:
                continue
            moved = jnp.roll(field, (step_row, step_col), axis=(1, 2))
            nearest = moved if nearest is None else jnp.maximum(nearest, moved)
    return nearest

def reference(shear, smoothing, offsets, thresholds):
    gamma = lax.complex(shear[0], shear[1])
    spectrum = jnp.fft.fft2(gamma, axes=(1, 2))
    freq_x = (jnp.fft.fftfreq(NX) * NX)[:, None]
    freq_y = (jnp.fft.fftfreq(NY) * NY)[None, :]
    square = jnp.maximum(freq_x * freq_x + freq_y * freq_y, 1.0)
    width = smoothing[:, None, None]
    damp = jnp.exp(-2.0 * math.pi ** 2 * width * width * ((freq_x / NX) ** 2 + (freq_y / NY) ** 2))
    kernel = lax.complex((freq_x * freq_x - freq_y * freq_y) / square * damp, -2.0 * freq_x * freq_y / square * damp)
    kappa = jnp.real(jnp.fft.ifft2(kernel * spectrum, axes=(1, 2)))
    rms = jnp.sqrt(lax.optimization_barrier(jnp.mean(kappa * kappa, axis=(1, 2))) + 1e-06)
    snr = kappa / rms[:, None, None]
    height_map = kappa - neighbour_max(kappa)
    full = jnp.repeat(jnp.repeat(offsets, CELL, axis=1), CELL, axis=2)
    code = (jnp.arange(NX, dtype=jnp.int32) % CELL)[:, None] * CELL + (jnp.arange(NY, dtype=jnp.int32) % CELL)[None, :]
    chosen = full == code[None]
    maps = kappa.shape[0]

    def pick(values):
        picked = jnp.where(chosen, values, 0.0)
        return picked.reshape(maps, NX // CELL, CELL, NY // CELL, CELL).sum(axis=(2, 4))
    heights = pick(height_map) / rms[:, None, None]
    values = pick(kappa) / rms[:, None, None]
    weight = jax.nn.sigmoid(heights / 0.05)
    levels = 0.25 * thresholds.astype(jnp.float32)
    above = jax.nn.sigmoid((values[..., None] - levels[:, None, None, :]) / 0.1)
    counts = lax.optimization_barrier(jnp.sum(weight[..., None] * above, axis=(1, 2)))
    return (snr, heights, counts)
```

```python
from functools import partial
import math

import jax
import jax.numpy as jnp
import numpy as np
from jax import lax
from jax.experimental import pallas as pl
from jax.experimental.pallas import tpu as pltpu
from jax.sharding import PartitionSpec as P

LANES = 128
CELL = 16
MESH = pl.DeviceIdType.MESH
GROUP = ("row", "col")
PEAK_SOFT = 0.05
BIN_SOFT = 0.1
BIN_STEP = 0.25


def split_table(values):
    values = jnp.asarray(values.astype(np.float32))
    high = values.astype(jnp.bfloat16)
    low = (values - high.astype(jnp.float32)).astype(jnp.bfloat16)
    return high, low


def split_value(x):
    high = x.astype(jnp.bfloat16)
    return high, (x - high.astype(jnp.float32)).astype(jnp.bfloat16)


def mm(a, b):
    dot = partial(jnp.dot, preferred_element_type=jnp.float32)
    return dot(a[0], b[0]) + (dot(a[0], b[1]) + dot(a[1], b[0]))


def y_tables(length):
    radix = length // LANES
    half = LANES // 2
    i = np.arange(LANES)[:, None].astype(np.float64)
    l = np.arange(LANES)[None, :].astype(np.float64)
    th = 2 * np.pi * ((i * l) % LANES) / LANES
    c, s = np.cos(th), np.sin(th)

    def order(re, im):
        return np.concatenate([re[:, :half], im[:, :half], re[:, half:], im[:, half:]], axis=1)

    base = np.concatenate([order(c, -s), order(s, c)], axis=0)
    inv = np.concatenate([order(c, -s), order(s, c)], axis=0).T * 2.0 / length
    th0 = 2 * np.pi * ((i * l[:, :half]) % LANES) / LANES
    th8 = 2 * np.pi * ((i * (radix // 2 + radix * l[:, :half])) % length) / length
    zero = np.zeros_like(th0)
    im0 = -np.sin(th0)
    im0[:, 0] = (-1.0) ** np.arange(LANES)
    top = np.concatenate([np.cos(th0), im0, zero, zero], axis=1)
    bottom = np.concatenate([zero, zero, np.cos(th8), -np.sin(th8)], axis=1)
    first = np.concatenate([top, bottom], axis=0)
    first_inv = first.T * 2.0 / length
    first_inv[0] /= 2.0
    first_inv[half] /= 2.0
    k = np.arange(radix // 2)[:, None].astype(np.float64)
    tw = 2 * np.pi * k * np.arange(LANES)[None, :] / length
    return base, first, inv, first_inv, np.cos(tw), np.sin(tw)


def x_tables(length):
    radix = length // LANES
    i = np.arange(LANES)[:, None].astype(np.float64)
    th = 2 * np.pi * ((i * i.T) % LANES) / LANES
    fwd = np.concatenate([np.cos(th), -np.sin(th)], axis=1)
    inv = np.concatenate([np.cos(th), np.sin(th)], axis=1) / length
    tw = 2 * np.pi * i * np.arange(radix)[None, :] / length
    return fwd, inv, np.concatenate([np.cos(tw), np.sin(tw)], axis=1)


def cs(k, n, radix):
    a = (k * n) % radix
    c, s = math.cos(2 * math.pi * a / radix), math.sin(2 * math.pi * a / radix)
    return round(c, 15), round(s, 15)


def axpy(total, coef, x):
    if coef == 0.0:
        return total
    if coef == 1.0:
        return x if total is None else total + x
    if coef == -1.0:
        return -x if total is None else total - x
    return coef * x if total is None else total + coef * x


def cos_sin_sums(parts):
    radix = len(parts)
    h = radix // 2
    plus = [None] + [parts[n] + parts[radix - n] for n in range(1, h)]
    minus = [None] + [parts[n] - parts[radix - n] for n in range(1, h)]
    pe, po = parts[0] + parts[h], parts[0] - parts[h]
    out = []
    for k in range(h // 2 + 1):
        ce = pe if k % 2 == 0 else po
        co = None
        se = so = None
        for n in range(1, h):
            c, s = cs(k, n, radix)
            if n % 2 == 0:
                ce = axpy(ce, c, plus[n])
                se = axpy(se, s, minus[n])
            else:
                co = axpy(co, c, plus[n])
                so = axpy(so, s, minus[n])
        out.append((ce, co, se, so))
    res = [None] * (h + 1)

    def add(a, b, sign):
        if a is None:
            return None if b is None else (b if sign > 0 else -b)
        if b is None:
            return a
        return a + b if sign > 0 else a - b

    for k in range(h // 2 + 1):
        ce, co, se, so = out[k]
        res[k] = (add(ce, co, 1), add(se, so, 1))
        if k != h - k:
            res[h - k] = (add(ce, co, -1), add(so, se, -1))
    return res


def forward_y_kernel(x_ref, bh, bl, fh, fl, tc, ts, out_ref):
    cols, rows, width = x_ref.shape[1:]
    per = width // LANES
    step = 32
    base, first = (bh[...], bl[...]), (fh[...], fl[...])
    for f in range(2):
        stage = []
        blocks = [x_ref[f, c, :, m * LANES : (m + 1) * LANES] for c in range(cols) for m in range(per)]
        sums = cos_sin_sums(blocks)
        h = len(blocks) // 2
        for k in range(h):
            if k == 0:
                both = jnp.concatenate([sums[0][0], sums[h][0]], axis=1)
                table = first
            else:
                re, im = sums[k][0], -sums[k][1]
                c, s = tc[k : k + 1, :], ts[k : k + 1, :]
                both = jnp.concatenate([re * c + im * s, im * c - re * s], axis=1)
                table = base
            got = mm(split_value(both), table)
            out_ref[2 * k, f] = got[:, :LANES]
            out_ref[2 * k + 1, f] = got[:, LANES:]


def turn(x, sign):
    return pltpu.roll(x, LANES // 2, 1) * sign


def middle_kernel(rows_total, x_ref, smooth_ref, fh, fl, ih, il, tw_ref, out_ref):
    length = rows_total
    radix = length // LANES
    h = radix // 2
    half = LANES // 2
    me = lax.axis_index("row") * lax.axis_size("col") + lax.axis_index("col")
    lane = lax.broadcasted_iota(jnp.int32, (LANES, LANES), 1)
    row = lax.broadcasted_iota(jnp.int32, (LANES, LANES), 0)
    sign = jnp.where(lane < half, -1.0, 1.0)
    slot = me * half + lane % half
    block, spot = slot // LANES, slot % LANES
    freq = jnp.where(
        block == 0,
        jnp.where(spot < half, radix * spot, h + radix * (spot - half)),
        block + radix * spot,
    )
    packed = slot == 0
    ky = jnp.where(freq < length // 2, freq, freq - length).astype(jnp.float32)
    one = [x_ref[n, 0] for n in range(radix)]
    two_raw = [x_ref[n, 1] for n in range(radix)]
    alternate = jnp.where(row % 2 == 0, 1.0, -1.0)
    total = two_raw[0]
    for n in range(1, radix):
        total = total + two_raw[n]
    corner = jnp.sum(total * alternate, axis=0, keepdims=True)
    two = [jnp.where(packed, -sign * a, b) for a, b in zip(one, two_raw)]
    sums = (cos_sin_sums(one), cos_sin_sums(two))
    fwd, inv = (fh[...], fl[...]), (ih[...], il[...])
    width = smooth_ref[0]
    scale = -2.0 * math.pi**2 * width * width
    edge = -float(length // 2)
    results = []
    for k in range(radix):
        j = min(k, radix - k)
        wc, ws = tw_ref[:, k : k + 1], tw_ref[:, radix + k : radix + k + 1]
        cols = []
        for f in range(2):
            c, s = sums[f][j]
            x = c
            if s is not None:
                x = c - turn(s, sign) if k == j else c + turn(s, sign)
            ix = turn(x, sign)
            if k:
                x, ix = wc * x - ws * ix, wc * ix + ws * x
            cols.append(jnp.concatenate([x, ix], axis=0))
        got = mm(fwd, split_value(jnp.concatenate(cols, axis=1)))
        g1, g2 = got[:, :LANES], got[:, LANES:]
        fx = k + radix * row
        kx = jnp.where(fx < length // 2, fx, fx - length).astype(jnp.float32)

        def kernel(ky):
            square = jnp.maximum(kx * kx + ky * ky, 1.0)
            damp = jnp.exp(scale * ((kx / length) ** 2 + (ky / length) ** 2))
            inverse = damp / square
            return (kx * kx - ky * ky) * inverse, -2.0 * kx * ky * inverse, damp

        kr, ki, _ = kernel(ky)
        nr, ni, damp_n = kernel(edge)
        last = fx == length // 2
        nr = jnp.where(last, 0.0, nr)
        ni_in = jnp.where(last, 0.0, ni)
        w1r = jnp.where(packed, 0.5 * (kr + nr), kr)
        w1i = jnp.where(packed, 0.5 * ni_in, jnp.where(last, ki, 0.0))
        w2r = jnp.where(packed, 0.5 * (kr - nr), jnp.where(last, 0.0, -ki))
        w2i = jnp.where(packed, -0.5 * ni_in, 0.0)
        z = w1r * g1 + w1i * turn(g1, sign) + w2r * g2 + w2i * turn(g2, sign)
        if k == 0:
            extra = jnp.where(packed & last & (lane >= half), -ni * corner, 0.0)
            z = z + extra
        iz = turn(z, sign)
        t = mm(inv, split_value(jnp.concatenate([z, iz], axis=0)))
        if k:
            t = wc * t + ws * turn(t, sign)
        results.append(t)
    sums = cos_sin_sums(results)
    for n in range(radix):
        j = min(n, radix - n)
        c, s = sums[j]
        x = c
        if s is not None:
            x = c + turn(s, sign) if n == j else c - turn(s, sign)
        out_ref[n] = x


def inverse_y_kernel(z_ref, bh, bl, fh, fl, tc, ts, out_ref, sq_ref, top_ref, bot_ref):
    count, rows, _ = z_ref.shape
    h = count // 2
    radix = count
    base, first = (bh[...], bl[...]), (fh[...], fl[...])
    real, imag = [None] * (h + 1), [None] * (h + 1)
    for k in range(h):
        both = jnp.concatenate([z_ref[2 * k], z_ref[2 * k + 1]], axis=1)
        got = mm(split_value(both), first if k == 0 else base)
        a, b = got[:, :LANES], got[:, LANES:]
        if k == 0:
            real[0], real[h] = a, b
        else:
            c, s = tc[k : k + 1, :], ts[k : k + 1, :]
            real[k], imag[k] = a * c - b * s, a * s + b * c
    square = None
    for n in range(h + 1):
        cosine, sine = real[0], None
        cosine = cosine + real[h] if n % 2 == 0 else cosine - real[h]
        for k in range(1, h):
            c, s = cs(k, n, radix)
            cosine = axpy(cosine, c, real[k])
            sine = axpy(sine, s, imag[k])
        for m in {n, (radix - n) % radix}:
            if sine is None:
                out = cosine
            else:
                out = cosine - sine if m == n else cosine + sine
            sl = slice(m * LANES, (m + 1) * LANES)
            out_ref[:, sl] = out
            top_ref[:, sl] = out[:1]
            bot_ref[:, sl] = out[rows - 1 :]
            sq = out * out
            square = sq if square is None else square + sq
    sq_ref[...] = jnp.sum(square, axis=0, keepdims=True)


def place():
    cols = lax.axis_size("col")
    count = lax.axis_size("row") * cols
    me = lax.axis_index("row") * cols + lax.axis_index("col")

    def at(d):
        peer = lax.rem(me + d, count)
        return {"row": peer // cols, "col": lax.rem(peer, cols)}

    return count, me, at


def greet(count, at):
    barrier = pltpu.get_barrier_semaphore()
    for d in range(1, count):
        pl.semaphore_signal(barrier, inc=1, device_id=at(d), device_id_type=MESH)
    pl.semaphore_wait(barrier, count - 1)


def spread(count, at, src, slots, send, recv):
    copies = []
    for d in range(1, count):
        copy = pltpu.make_async_remote_copy(
            src_ref=src, dst_ref=slots.at[d - 1], send_sem=send.at[d - 1],
            recv_sem=recv.at[d - 1], device_id=at(d), device_id_type=MESH,
        )
        copy.start()
        copies.append(copy)
    return copies


def sum_kernel(x_ref, out_ref, slots, send, recv):
    count, _, at = place()
    greet(count, at)
    for copy in spread(count, at, x_ref, slots, send, recv):
        copy.wait()
    total = x_ref[...]
    for d in range(1, count):
        total = total + slots[d - 1]
    out_ref[...] = total


def edge_kernel(sq_ref, top_ref, bot_ref, out_ref, above_ref, below_ref, slots, send, recv, hsend, hrecv):
    count, _, at = place()
    greet(count, at)
    copies = spread(count, at, sq_ref, slots, send, recv)
    for i, (src, dst, d) in enumerate(((bot_ref, above_ref, 1), (top_ref, below_ref, count - 1))):
        copy = pltpu.make_async_remote_copy(
            src_ref=src, dst_ref=dst, send_sem=hsend.at[i], recv_sem=hrecv.at[i],
            device_id=at(d), device_id_type=MESH,
        )
        copy.start()
        copies.append(copy)
    for copy in copies:
        copy.wait()
    total = sq_ref[...]
    for d in range(1, count):
        total = total + slots[d - 1]
    out_ref[...] = total


def peak_kernel(pixels, x_ref, above_ref, below_ref, sq_ref, off_ref, thr_ref, snr_ref, high_ref, cnt_ref, wide):
    rows, width = x_ref.shape
    cells = width // CELL
    pad = 8
    rms = jnp.sqrt(jnp.sum(sq_ref[...], axis=1, keepdims=True) / pixels + 1e-06)

    def three(x):
        side = jnp.maximum(pltpu.roll(x, 1, 1), pltpu.roll(x, width - 1, 1))
        return side, jnp.maximum(side, x)

    wide[pad - 1 : pad, :] = three(jnp.broadcast_to(above_ref[...], (8, width)))[1][:1]
    wide[pad + rows : pad + rows + 1, :] = three(jnp.broadcast_to(below_ref[...], (8, width)))[1][:1]
    for p in range(rows // CELL):
        sl = slice(p * CELL, (p + 1) * CELL)
        wide[pad + p * CELL : pad + (p + 1) * CELL, :] = three(x_ref[sl, :])[1]
    same = lax.broadcasted_iota(jnp.int32, (cells, width), 1) // CELL == lax.broadcasted_iota(
        jnp.int32, (cells, width), 0
    )
    spread_table = same.astype(jnp.bfloat16)
    full = jnp.dot(
        off_ref[...].astype(jnp.bfloat16), spread_table, preferred_element_type=jnp.float32
    ).astype(jnp.int32)
    code = lax.broadcasted_iota(jnp.int32, (CELL, width), 0) * CELL + (
        lax.broadcasted_iota(jnp.int32, (CELL, width), 1) % CELL
    )
    tops, mids = [], []
    for p in range(rows // CELL):
        low = pad + p * CELL
        x = x_ref[p * CELL : (p + 1) * CELL, :]
        snr_ref[p * CELL : (p + 1) * CELL, :] = x / rms
        near = jnp.maximum(
            three(x)[0],
            jnp.maximum(wide[low - 1 : low - 1 + CELL, :], wide[low + 1 : low + 1 + CELL, :]),
        )
        chosen = full[p : p + 1, :] == code
        tops.append(jnp.sum(jnp.where(chosen, x - near, 0.0), axis=0, keepdims=True))
        mids.append(jnp.sum(jnp.where(chosen, x, 0.0), axis=0, keepdims=True))

    def gather(parts):
        dot = partial(
            lax.dot_general, dimension_numbers=(((1,), (1,)), ((), ())),
            preferred_element_type=jnp.float32,
        )
        x = jnp.concatenate(parts, axis=0)
        a = x.astype(jnp.bfloat16)
        rest = x - a.astype(jnp.float32)
        b = rest.astype(jnp.bfloat16)
        c = (rest - b.astype(jnp.float32)).astype(jnp.bfloat16)
        return dot(a, spread_table) + (dot(b, spread_table) + dot(c, spread_table))

    heights = gather(tops) / rms
    values = gather(mids) / rms
    high_ref[...] = heights
    weight = 1.0 / (1.0 + jnp.exp(-heights / PEAK_SOFT))
    lane = lax.broadcasted_iota(jnp.int32, (1, LANES), 1)
    counts = jnp.zeros((1, LANES), jnp.float32)
    for k in range(thr_ref.shape[0]):
        level = BIN_STEP * thr_ref[k].astype(jnp.float32)
        above = weight / (1.0 + jnp.exp((level - values) / BIN_SOFT))
        one = jnp.sum(jnp.sum(above, axis=0, keepdims=True), axis=1, keepdims=True)
        counts = jnp.where(lane == k, one, counts)
    cnt_ref[...] = counts


VM = pl.BlockSpec(memory_space=pltpu.VMEM)
SM = pl.BlockSpec(memory_space=pltpu.SMEM)
F32 = jnp.float32


def shape(*dims):
    return jax.ShapeDtypeStruct(dims, F32)


def call(kernel, out_shape, specs, scratch=(), **params):
    outs = out_shape if isinstance(out_shape, tuple) else None
    return pl.pallas_call(
        kernel,
        out_shape=out_shape,
        in_specs=specs,
        out_specs=VM if outs is None else tuple(VM for _ in outs),
        scratch_shapes=list(scratch),
        compiler_params=pltpu.CompilerParams(vmem_limit_bytes=40 * 2**20, **params),
    )


def one_map(shear, smoothing, offsets, thresholds):
    rows_in, cols_in = shear.shape[1:]
    nrow, ncol = lax.axis_size("row"), lax.axis_size("col")
    nx, ny = rows_in * nrow, cols_in * ncol
    count = nrow * ncol
    rows = nx // count
    base, first, inv, first_inv, tc, ts = y_tables(ny)
    fwd_x, inv_x, tw_x = x_tables(nx)
    tc, ts, tw_x = (jnp.asarray(t.astype(np.float32)) for t in (tc, ts, tw_x))
    x = shear.reshape(2, ncol, rows, cols_in)
    x = lax.all_to_all(x, "col", split_axis=1, concat_axis=1, tiled=True)
    x = call(forward_y_kernel, shape(count, 2, rows, LANES), [VM] * 7)(
        x, *split_table(base), *split_table(first), tc, ts
    )
    x = lax.all_to_all(x, GROUP, split_axis=0, concat_axis=0, tiled=True)
    x = call(partial(middle_kernel, nx), shape(count, rows, LANES), [VM, SM] + [VM] * 5)(
        x, smoothing, *split_table(fwd_x), *split_table(inv_x), tw_x
    )
    x = lax.all_to_all(x, GROUP, split_axis=0, concat_axis=0, tiled=True)
    kappa, sq, top, bot = call(
        inverse_y_kernel,
        (shape(rows, ny), shape(1, LANES), shape(1, ny), shape(1, ny)),
        [VM] * 7,
    )(x, *split_table(inv), *split_table(first_inv), tc, ts)
    dma = pltpu.SemaphoreType.DMA
    slots = [pltpu.VMEM((count - 1, 1, LANES), F32), dma((count - 1,)), dma((count - 1,))]
    sq, above, below = call(
        edge_kernel,
        (shape(1, LANES), shape(1, ny), shape(1, ny)),
        [VM] * 3,
        slots + [dma((2,)), dma((2,))],
        collective_id=0,
        has_side_effects=True,
    )(sq, top, bot)
    snr, heights, local = call(
        partial(peak_kernel, float(nx * ny)),
        (shape(rows, ny), shape(*offsets.shape), shape(1, LANES)),
        [VM] * 5 + [SM],
        [pltpu.VMEM((rows + 16, ny), F32)],
    )(kappa, above, below, sq, offsets, thresholds)
    counts = call(
        sum_kernel, shape(1, LANES), [VM], slots, collective_id=1, has_side_effects=True
    )(local)
    return snr, heights, counts[0, : thresholds.shape[0]]


def body(shear, smoothing, offsets, thresholds):
    outs = [
        one_map(shear[:, m], smoothing[m : m + 1], offsets[m], thresholds[m])
        for m in range(shear.shape[1])
    ]
    return tuple(jnp.stack(parts) for parts in zip(*outs))


def solution(mesh):
    return jax.shard_map(
        body,
        mesh=mesh,
        in_specs=(
            P(None, "maps", "row", "col"),
            P("maps"),
            P("maps", GROUP, None),
            P("maps", None),
        ),
        out_specs=(P("maps", GROUP, None), P("maps", GROUP, None), P("maps", None)),
        check_vma=False,
    )
```

```python
from functools import partial
import math

import jax
import jax.numpy as jnp
import numpy as np
from jax import lax
from jax.experimental import pallas as pl
from jax.experimental.pallas import tpu as pltpu
from jax.sharding import PartitionSpec as P

LANES = 128
CELL = 16
MESH = pl.DeviceIdType.MESH
GROUP = ("row", "col")
PEAK_SOFT = 0.05
BIN_SOFT = 0.1
BIN_STEP = 0.25


def split_table(values):
    values = jnp.asarray(values.astype(np.float32))
    high = values.astype(jnp.bfloat16)
    low = (values - high.astype(jnp.float32)).astype(jnp.bfloat16)
    return high, low


def split_value(x):
    high = x.astype(jnp.bfloat16)
    return high, (x - high.astype(jnp.float32)).astype(jnp.bfloat16)


def mm(a, b):
    dot = partial(jnp.dot, preferred_element_type=jnp.float32)
    return dot(a[0], b[0]) + (dot(a[0], b[1]) + dot(a[1], b[0]))


def y_tables(length):
    radix = length // LANES
    half = LANES // 2
    i = np.arange(LANES)[:, None].astype(np.float64)
    l = np.arange(LANES)[None, :].astype(np.float64)
    th = 2 * np.pi * ((i * l) % LANES) / LANES
    c, s = np.cos(th), np.sin(th)

    def order(re, im):
        return np.concatenate([re[:, :half], im[:, :half], re[:, half:], im[:, half:]], axis=1)

    base = np.concatenate([order(c, -s), order(s, c)], axis=0)
    inv = np.concatenate([order(c, -s), order(s, c)], axis=0).T * 2.0 / length
    th0 = 2 * np.pi * ((i * l[:, :half]) % LANES) / LANES
    th8 = 2 * np.pi * ((i * (radix // 2 + radix * l[:, :half])) % length) / length
    zero = np.zeros_like(th0)
    im0 = -np.sin(th0)
    im0[:, 0] = (-1.0) ** np.arange(LANES)
    top = np.concatenate([np.cos(th0), im0, zero, zero], axis=1)
    bottom = np.concatenate([zero, zero, np.cos(th8), -np.sin(th8)], axis=1)
    first = np.concatenate([top, bottom], axis=0)
    first_inv = first.T * 2.0 / length
    first_inv[0] /= 2.0
    first_inv[half] /= 2.0
    k = np.arange(radix // 2)[:, None].astype(np.float64)
    tw = 2 * np.pi * k * np.arange(LANES)[None, :] / length
    return base, first, inv, first_inv, np.cos(tw), np.sin(tw)


def x_tables(length):
    radix = length // LANES
    i = np.arange(LANES)[:, None].astype(np.float64)
    th = 2 * np.pi * ((i * i.T) % LANES) / LANES
    fwd = np.concatenate([np.cos(th), -np.sin(th)], axis=1)
    inv = np.concatenate([np.cos(th), np.sin(th)], axis=1) / length
    tw = 2 * np.pi * i * np.arange(radix)[None, :] / length
    return fwd, inv, np.concatenate([np.cos(tw), np.sin(tw)], axis=1)


def cs(k, n, radix):
    a = (k * n) % radix
    c, s = math.cos(2 * math.pi * a / radix), math.sin(2 * math.pi * a / radix)
    return round(c, 15), round(s, 15)


def axpy(total, coef, x):
    if coef == 0.0:
        return total
    if coef == 1.0:
        return x if total is None else total + x
    if coef == -1.0:
        return -x if total is None else total - x
    return coef * x if total is None else total + coef * x


def cos_sin_sums(parts):
    radix = len(parts)
    h = radix // 2
    plus = [None] + [parts[n] + parts[radix - n] for n in range(1, h)]
    minus = [None] + [parts[n] - parts[radix - n] for n in range(1, h)]
    pe, po = parts[0] + parts[h], parts[0] - parts[h]
    out = []
    for k in range(h // 2 + 1):
        ce = pe if k % 2 == 0 else po
        co = None
        se = so = None
        for n in range(1, h):
            c, s = cs(k, n, radix)
            if n % 2 == 0:
                ce = axpy(ce, c, plus[n])
                se = axpy(se, s, minus[n])
            else:
                co = axpy(co, c, plus[n])
                so = axpy(so, s, minus[n])
        out.append((ce, co, se, so))
    res = [None] * (h + 1)

    def add(a, b, sign):
        if a is None:
            return None if b is None else (b if sign > 0 else -b)
        if b is None:
            return a
        return a + b if sign > 0 else a - b

    for k in range(h // 2 + 1):
        ce, co, se, so = out[k]
        res[k] = (add(ce, co, 1), add(se, so, 1))
        if k != h - k:
            res[h - k] = (add(ce, co, -1), add(so, se, -1))
    return res


def masked(index, size, m):
    assert size == 4
    return (index, index + 1 - 2 * lax.rem(index, 2), lax.rem(index + 2, 4), 3 - index)[m]


def partners():
    nrow, ncol = lax.axis_size("row"), lax.axis_size("col")
    far = list(range(ncol // 2, ncol)) + list(range(ncol // 2))
    return [(p, q) for q in far for p in reversed(range(nrow))]


def seat(p, q):
    row = masked(lax.axis_index("row"), lax.axis_size("row"), p)
    col = masked(lax.axis_index("col"), lax.axis_size("col"), q)
    return row, col, row * lax.axis_size("col") + col


def deal(src_of, dst, send, recv, local):
    _, me, _ = place()
    copies = []
    own = pltpu.make_async_copy(src_of(me), dst, local)
    own.start()
    for i, (p, q) in enumerate(partners()):
        row, col, peer = seat(p, q)
        if p == 0 and q == 0:
            continue
        copy = pltpu.make_async_remote_copy(
            src_ref=src_of(peer), dst_ref=dst, send_sem=send.at[i], recv_sem=recv.at[i],
            device_id={"row": row, "col": col}, device_id_type=MESH,
        )
        copy.start()
        copies.append(copy)
    return copies + [own]


def forward_y_kernel(shear, bh, bl, fh, fl, tc, ts, out_ref, xbuf, sbuf, asend, arecv, bsend, brecv, loc):
    _, cols, rows, width = xbuf.shape
    per = width // LANES
    count, me, at = place()
    greet(count, at)
    here = lax.axis_index("col")
    arrive = []
    for f in range(2):
        copies = []
        for q in list(range(cols // 2, cols)) + list(range(cols // 2)):
            other = masked(here, cols, q)
            src = shear.at[f, pl.ds(pl.multiple_of(other * rows, rows), rows), :]
            dst = xbuf.at[f, here]
            if q == 0:
                copy = pltpu.make_async_copy(src, dst, loc.at[f])
            else:
                copy = pltpu.make_async_remote_copy(
                    src_ref=src, dst_ref=dst, send_sem=asend.at[f, q], recv_sem=arecv.at[f, q],
                    device_id={"col": other}, device_id_type=MESH,
                )
            copy.start()
            copies.append(copy)
        arrive.append(copies)
    base, first = (bh[...], bl[...]), (fh[...], fl[...])
    leave = []
    for f in range(2):
        for copy in arrive[f]:
            copy.wait()
        blocks = [xbuf[f, c, :, m * LANES : (m + 1) * LANES] for c in range(cols) for m in range(per)]
        sums = cos_sin_sums(blocks)
        h = len(blocks) // 2
        for k in range(h):
            if k == 0:
                both = jnp.concatenate([sums[0][0], sums[h][0]], axis=1)
                table = first
            else:
                re, im = sums[k][0], -sums[k][1]
                c, s = tc[k : k + 1, :], ts[k : k + 1, :]
                both = jnp.concatenate([re * c + im * s, im * c - re * s], axis=1)
                table = base
            got = mm(split_value(both), table)
            sbuf[2 * k, f] = got[:, :LANES]
            sbuf[2 * k + 1, f] = got[:, LANES:]
        leave += deal(
            lambda peer, f=f: sbuf.at[peer, f], out_ref.at[me, f], bsend.at[f], brecv.at[f], loc.at[2 + f]
        )
    for copy in leave:
        copy.wait()


def turn(x, sign):
    return pltpu.roll(x, LANES // 2, 1) * sign


def middle_kernel(rows_total, x_ref, smooth_ref, fh, fl, ih, il, tw_ref, out_ref, sbuf, send, recv, loc):
    length = rows_total
    radix = length // LANES
    h = radix // 2
    half = LANES // 2
    count, me, at = place()
    greet(count, at)
    lane = lax.broadcasted_iota(jnp.int32, (LANES, LANES), 1)
    row = lax.broadcasted_iota(jnp.int32, (LANES, LANES), 0)
    sign = jnp.where(lane < half, -1.0, 1.0)
    slot = me * half + lane % half
    block, spot = slot // LANES, slot % LANES
    freq = jnp.where(
        block == 0,
        jnp.where(spot < half, radix * spot, h + radix * (spot - half)),
        block + radix * spot,
    )
    packed = slot == 0
    ky = jnp.where(freq < length // 2, freq, freq - length).astype(jnp.float32)
    one = [x_ref[n, 0] for n in range(radix)]
    two_raw = [x_ref[n, 1] for n in range(radix)]
    alternate = jnp.where(row % 2 == 0, 1.0, -1.0)
    total = two_raw[0]
    for n in range(1, radix):
        total = total + two_raw[n]
    corner = jnp.sum(total * alternate, axis=0, keepdims=True)
    two = [jnp.where(packed, -sign * a, b) for a, b in zip(one, two_raw)]
    sums = (cos_sin_sums(one), cos_sin_sums(two))
    fwd, inv = (fh[...], fl[...]), (ih[...], il[...])
    width = smooth_ref[0]
    scale = -2.0 * math.pi**2 * width * width
    edge = -float(length // 2)
    results = []
    for k in range(radix):
        j = min(k, radix - k)
        wc, ws = tw_ref[:, k : k + 1], tw_ref[:, radix + k : radix + k + 1]
        cols = []
        for f in range(2):
            c, s = sums[f][j]
            x = c
            if s is not None:
                x = c - turn(s, sign) if k == j else c + turn(s, sign)
            ix = turn(x, sign)
            if k:
                x, ix = wc * x - ws * ix, wc * ix + ws * x
            cols.append(jnp.concatenate([x, ix], axis=0))
        got = mm(fwd, split_value(jnp.concatenate(cols, axis=1)))
        g1, g2 = got[:, :LANES], got[:, LANES:]
        fx = k + radix * row
        kx = jnp.where(fx < length // 2, fx, fx - length).astype(jnp.float32)

        def kernel(ky):
            square = jnp.maximum(kx * kx + ky * ky, 1.0)
            damp = jnp.exp(scale * ((kx / length) ** 2 + (ky / length) ** 2))
            inverse = damp / square
            return (kx * kx - ky * ky) * inverse, -2.0 * kx * ky * inverse, damp

        kr, ki, _ = kernel(ky)
        nr, ni, damp_n = kernel(edge)
        last = fx == length // 2
        nr = jnp.where(last, 0.0, nr)
        ni_in = jnp.where(last, 0.0, ni)
        w1r = jnp.where(packed, 0.5 * (kr + nr), kr)
        w1i = jnp.where(packed, 0.5 * ni_in, jnp.where(last, ki, 0.0))
        w2r = jnp.where(packed, 0.5 * (kr - nr), jnp.where(last, 0.0, -ki))
        w2i = jnp.where(packed, -0.5 * ni_in, 0.0)
        z = w1r * g1 + w1i * turn(g1, sign) + w2r * g2 + w2i * turn(g2, sign)
        if k == 0:
            extra = jnp.where(packed & last & (lane >= half), -ni * corner, 0.0)
            z = z + extra
        iz = turn(z, sign)
        t = mm(inv, split_value(jnp.concatenate([z, iz], axis=0)))
        if k:
            t = wc * t + ws * turn(t, sign)
        results.append(t)
    sums = cos_sin_sums(results)
    for n in range(radix):
        j = min(n, radix - n)
        c, s = sums[j]
        x = c
        if s is not None:
            x = c + turn(s, sign) if n == j else c - turn(s, sign)
        sbuf[n] = x
    for copy in deal(lambda peer: sbuf.at[peer], out_ref.at[me], send, recv, loc.at[0]):
        copy.wait()


def inverse_y_kernel(z_ref, bh, bl, fh, fl, tc, ts, out_ref, sq_ref, top_ref, bot_ref):
    count, rows, _ = z_ref.shape
    h = count // 2
    radix = count
    base, first = (bh[...], bl[...]), (fh[...], fl[...])
    real, imag = [None] * (h + 1), [None] * (h + 1)
    for k in range(h):
        both = jnp.concatenate([z_ref[2 * k], z_ref[2 * k + 1]], axis=1)
        got = mm(split_value(both), first if k == 0 else base)
        a, b = got[:, :LANES], got[:, LANES:]
        if k == 0:
            real[0], real[h] = a, b
        else:
            c, s = tc[k : k + 1, :], ts[k : k + 1, :]
            real[k], imag[k] = a * c - b * s, a * s + b * c
    square = None
    for n in range(h + 1):
        cosine, sine = real[0], None
        cosine = cosine + real[h] if n % 2 == 0 else cosine - real[h]
        for k in range(1, h):
            c, s = cs(k, n, radix)
            cosine = axpy(cosine, c, real[k])
            sine = axpy(sine, s, imag[k])
        for m in {n, (radix - n) % radix}:
            if sine is None:
                out = cosine
            else:
                out = cosine - sine if m == n else cosine + sine
            sl = slice(m * LANES, (m + 1) * LANES)
            out_ref[:, sl] = out
            top_ref[:, sl] = out[:1]
            bot_ref[:, sl] = out[rows - 1 :]
            sq = out * out
            square = sq if square is None else square + sq
    sq_ref[...] = jnp.sum(square, axis=0, keepdims=True)


def place():
    cols = lax.axis_size("col")
    count = lax.axis_size("row") * cols
    me = lax.axis_index("row") * cols + lax.axis_index("col")

    def at(d):
        peer = lax.rem(me + d, count)
        return {"row": peer // cols, "col": lax.rem(peer, cols)}

    return count, me, at


def greet(count, at):
    barrier = pltpu.get_barrier_semaphore()
    for d in range(1, count):
        pl.semaphore_signal(barrier, inc=1, device_id=at(d), device_id_type=MESH)
    pl.semaphore_wait(barrier, count - 1)


def spread(count, at, src, slots, send, recv):
    copies = []
    for d in range(1, count):
        copy = pltpu.make_async_remote_copy(
            src_ref=src, dst_ref=slots.at[d - 1], send_sem=send.at[d - 1],
            recv_sem=recv.at[d - 1], device_id=at(d), device_id_type=MESH,
        )
        copy.start()
        copies.append(copy)
    return copies


def sum_kernel(x_ref, out_ref, slots, send, recv):
    count, _, at = place()
    greet(count, at)
    for copy in spread(count, at, x_ref, slots, send, recv):
        copy.wait()
    total = x_ref[...]
    for d in range(1, count):
        total = total + slots[d - 1]
    out_ref[...] = total


def edge_kernel(sq_ref, top_ref, bot_ref, out_ref, above_ref, below_ref, slots, send, recv, hsend, hrecv):
    count, _, at = place()
    greet(count, at)
    copies = spread(count, at, sq_ref, slots, send, recv)
    for i, (src, dst, d) in enumerate(((bot_ref, above_ref, 1), (top_ref, below_ref, count - 1))):
        copy = pltpu.make_async_remote_copy(
            src_ref=src, dst_ref=dst, send_sem=hsend.at[i], recv_sem=hrecv.at[i],
            device_id=at(d), device_id_type=MESH,
        )
        copy.start()
        copies.append(copy)
    for copy in copies:
        copy.wait()
    total = sq_ref[...]
    for d in range(1, count):
        total = total + slots[d - 1]
    out_ref[...] = total


def peak_kernel(pixels, x_ref, above_ref, below_ref, sq_ref, off_ref, thr_ref, snr_ref, high_ref, cnt_ref, wide):
    rows, width = x_ref.shape
    cells = width // CELL
    pad = 8
    rms = jnp.sqrt(jnp.sum(sq_ref[...], axis=1, keepdims=True) / pixels + 1e-06)

    def three(x):
        side = jnp.maximum(pltpu.roll(x, 1, 1), pltpu.roll(x, width - 1, 1))
        return side, jnp.maximum(side, x)

    wide[pad - 1 : pad, :] = three(jnp.broadcast_to(above_ref[...], (8, width)))[1][:1]
    wide[pad + rows : pad + rows + 1, :] = three(jnp.broadcast_to(below_ref[...], (8, width)))[1][:1]
    for p in range(rows // CELL):
        sl = slice(p * CELL, (p + 1) * CELL)
        wide[pad + p * CELL : pad + (p + 1) * CELL, :] = three(x_ref[sl, :])[1]
    same = lax.broadcasted_iota(jnp.int32, (cells, width), 1) // CELL == lax.broadcasted_iota(
        jnp.int32, (cells, width), 0
    )
    spread_table = same.astype(jnp.bfloat16)
    full = jnp.dot(
        off_ref[...].astype(jnp.bfloat16), spread_table, preferred_element_type=jnp.float32
    ).astype(jnp.int32)
    code = lax.broadcasted_iota(jnp.int32, (CELL, width), 0) * CELL + (
        lax.broadcasted_iota(jnp.int32, (CELL, width), 1) % CELL
    )
    tops, mids = [], []
    for p in range(rows // CELL):
        low = pad + p * CELL
        x = x_ref[p * CELL : (p + 1) * CELL, :]
        snr_ref[p * CELL : (p + 1) * CELL, :] = x / rms
        near = jnp.maximum(
            three(x)[0],
            jnp.maximum(wide[low - 1 : low - 1 + CELL, :], wide[low + 1 : low + 1 + CELL, :]),
        )
        chosen = full[p : p + 1, :] == code
        tops.append(jnp.sum(jnp.where(chosen, x - near, 0.0), axis=0, keepdims=True))
        mids.append(jnp.sum(jnp.where(chosen, x, 0.0), axis=0, keepdims=True))

    def gather(parts):
        dot = partial(
            lax.dot_general, dimension_numbers=(((1,), (1,)), ((), ())),
            preferred_element_type=jnp.float32,
        )
        x = jnp.concatenate(parts, axis=0)
        a = x.astype(jnp.bfloat16)
        rest = x - a.astype(jnp.float32)
        b = rest.astype(jnp.bfloat16)
        c = (rest - b.astype(jnp.float32)).astype(jnp.bfloat16)
        return dot(a, spread_table) + (dot(b, spread_table) + dot(c, spread_table))

    heights = gather(tops) / rms
    values = gather(mids) / rms
    high_ref[...] = heights
    weight = 1.0 / (1.0 + jnp.exp(-heights / PEAK_SOFT))
    lane = lax.broadcasted_iota(jnp.int32, (1, LANES), 1)
    counts = jnp.zeros((1, LANES), jnp.float32)
    for k in range(thr_ref.shape[0]):
        level = BIN_STEP * thr_ref[k].astype(jnp.float32)
        above = weight / (1.0 + jnp.exp((level - values) / BIN_SOFT))
        one = jnp.sum(jnp.sum(above, axis=0, keepdims=True), axis=1, keepdims=True)
        counts = jnp.where(lane == k, one, counts)
    cnt_ref[...] = counts


VM = pl.BlockSpec(memory_space=pltpu.VMEM)
SM = pl.BlockSpec(memory_space=pltpu.SMEM)
F32 = jnp.float32


def shape(*dims):
    return jax.ShapeDtypeStruct(dims, F32)


def call(kernel, out_shape, specs, scratch=(), **params):
    outs = out_shape if isinstance(out_shape, tuple) else None
    return pl.pallas_call(
        kernel,
        out_shape=out_shape,
        in_specs=specs,
        out_specs=VM if outs is None else tuple(VM for _ in outs),
        scratch_shapes=list(scratch),
        compiler_params=pltpu.CompilerParams(vmem_limit_bytes=40 * 2**20, **params),
    )


def one_map(shear, smoothing, offsets, thresholds):
    rows_in, cols_in = shear.shape[1:]
    nrow, ncol = lax.axis_size("row"), lax.axis_size("col")
    nx, ny = rows_in * nrow, cols_in * ncol
    count = nrow * ncol
    rows = nx // count
    base, first, inv, first_inv, tc, ts = y_tables(ny)
    fwd_x, inv_x, tw_x = x_tables(nx)
    tc, ts, tw_x = (jnp.asarray(t.astype(np.float32)) for t in (tc, ts, tw_x))
    dma = pltpu.SemaphoreType.DMA
    x = call(
        forward_y_kernel,
        shape(count, 2, rows, LANES),
        [pl.BlockSpec(memory_space=pl.ANY)] + [VM] * 6,
        [
            pltpu.VMEM((2, ncol, rows, cols_in), F32),
            pltpu.VMEM((count, 2, rows, LANES), F32),
            dma((2, ncol)), dma((2, ncol)), dma((2, count)), dma((2, count)), dma((4,)),
        ],
        collective_id=2,
        has_side_effects=True,
    )(shear, *split_table(base), *split_table(first), tc, ts)
    x = call(
        partial(middle_kernel, nx),
        shape(count, rows, LANES),
        [VM, SM] + [VM] * 5,
        [pltpu.VMEM((count, rows, LANES), F32), dma((count,)), dma((count,)), dma((1,))],
        collective_id=3,
        has_side_effects=True,
    )(x, smoothing, *split_table(fwd_x), *split_table(inv_x), tw_x)
    kappa, sq, top, bot = call(
        inverse_y_kernel,
        (shape(rows, ny), shape(1, LANES), shape(1, ny), shape(1, ny)),
        [VM] * 7,
    )(x, *split_table(inv), *split_table(first_inv), tc, ts)
    slots = [pltpu.VMEM((count - 1, 1, LANES), F32), dma((count - 1,)), dma((count - 1,))]
    sq, above, below = call(
        edge_kernel,
        (shape(1, LANES), shape(1, ny), shape(1, ny)),
        [VM] * 3,
        slots + [dma((2,)), dma((2,))],
        collective_id=0,
        has_side_effects=True,
    )(sq, top, bot)
    snr, heights, local = call(
        partial(peak_kernel, float(nx * ny)),
        (shape(rows, ny), shape(*offsets.shape), shape(1, LANES)),
        [VM] * 5 + [SM],
        [pltpu.VMEM((rows + 16, ny), F32)],
    )(kappa, above, below, sq, offsets, thresholds)
    counts = call(
        sum_kernel, shape(1, LANES), [VM], slots, collective_id=1, has_side_effects=True
    )(local)
    return snr, heights, counts[0, : thresholds.shape[0]]


def body(shear, smoothing, offsets, thresholds):
    outs = [
        one_map(shear[:, m], smoothing[m : m + 1], offsets[m], thresholds[m])
        for m in range(shear.shape[1])
    ]
    return tuple(jnp.stack(parts) for parts in zip(*outs))


def solution(mesh):
    return jax.shard_map(
        body,
        mesh=mesh,
        in_specs=(
            P(None, "maps", "row", "col"),
            P("maps"),
            P("maps", GROUP, None),
            P("maps", None),
        ),
        out_specs=(P("maps", GROUP, None), P("maps", GROUP, None), P("maps", None)),
        check_vma=False,
    )
```

```python
from functools import partial
import math

import jax
import jax.numpy as jnp
import numpy as np
from jax import lax
from jax.experimental import pallas as pl
from jax.experimental.pallas import tpu as pltpu
from jax.sharding import PartitionSpec as P

LANES = 128
CELL = 16
MESH = pl.DeviceIdType.MESH
GROUP = ("row", "col")
PEAK_SOFT = 0.05
BIN_SOFT = 0.1
BIN_STEP = 0.25


def split_table(values):
    values = jnp.asarray(values.astype(np.float32))
    high = values.astype(jnp.bfloat16)
    low = (values - high.astype(jnp.float32)).astype(jnp.bfloat16)
    return high, low


def split_value(x):
    high = x.astype(jnp.bfloat16)
    return high, (x - high.astype(jnp.float32)).astype(jnp.bfloat16)


def mm(a, b):
    dot = partial(jnp.dot, preferred_element_type=jnp.float32)
    return dot(a[0], b[0]) + (dot(a[0], b[1]) + dot(a[1], b[0]))


def y_tables(length):
    radix = length // LANES
    half = LANES // 2
    i = np.arange(LANES)[:, None].astype(np.float64)
    l = np.arange(LANES)[None, :].astype(np.float64)
    th = 2 * np.pi * ((i * l) % LANES) / LANES
    c, s = np.cos(th), np.sin(th)

    def order(re, im):
        return np.concatenate([re[:, :half], im[:, :half], re[:, half:], im[:, half:]], axis=1)

    base = np.concatenate([order(c, -s), order(s, c)], axis=0)
    inv = np.concatenate([order(c, -s), order(s, c)], axis=0).T * 2.0 / length
    th0 = 2 * np.pi * ((i * l[:, :half]) % LANES) / LANES
    th8 = 2 * np.pi * ((i * (radix // 2 + radix * l[:, :half])) % length) / length
    zero = np.zeros_like(th0)
    im0 = -np.sin(th0)
    im0[:, 0] = (-1.0) ** np.arange(LANES)
    top = np.concatenate([np.cos(th0), im0, zero, zero], axis=1)
    bottom = np.concatenate([zero, zero, np.cos(th8), -np.sin(th8)], axis=1)
    first = np.concatenate([top, bottom], axis=0)
    first_inv = first.T * 2.0 / length
    first_inv[0] /= 2.0
    first_inv[half] /= 2.0
    k = np.arange(radix // 2)[:, None].astype(np.float64)
    tw = 2 * np.pi * k * np.arange(LANES)[None, :] / length
    return base, first, inv, first_inv, np.cos(tw), np.sin(tw)


def x_tables(length):
    radix = length // LANES
    i = np.arange(LANES)[:, None].astype(np.float64)
    th = 2 * np.pi * ((i * i.T) % LANES) / LANES
    fwd = np.concatenate([np.cos(th), -np.sin(th)], axis=1)
    inv = np.concatenate([np.cos(th), np.sin(th)], axis=1) / length
    tw = 2 * np.pi * i * np.arange(radix)[None, :] / length
    return fwd, inv, np.concatenate([np.cos(tw), np.sin(tw)], axis=1)


def cs(k, n, radix):
    a = (k * n) % radix
    c, s = math.cos(2 * math.pi * a / radix), math.sin(2 * math.pi * a / radix)
    return round(c, 15), round(s, 15)


def axpy(total, coef, x):
    if coef == 0.0:
        return total
    if coef == 1.0:
        return x if total is None else total + x
    if coef == -1.0:
        return -x if total is None else total - x
    return coef * x if total is None else total + coef * x


def cos_sin_sums(parts):
    radix = len(parts)
    h = radix // 2
    plus = [None] + [parts[n] + parts[radix - n] for n in range(1, h)]
    minus = [None] + [parts[n] - parts[radix - n] for n in range(1, h)]
    pe, po = parts[0] + parts[h], parts[0] - parts[h]
    out = []
    for k in range(h // 2 + 1):
        ce = pe if k % 2 == 0 else po
        co = None
        se = so = None
        for n in range(1, h):
            c, s = cs(k, n, radix)
            if n % 2 == 0:
                ce = axpy(ce, c, plus[n])
                se = axpy(se, s, minus[n])
            else:
                co = axpy(co, c, plus[n])
                so = axpy(so, s, minus[n])
        out.append((ce, co, se, so))
    res = [None] * (h + 1)

    def add(a, b, sign):
        if a is None:
            return None if b is None else (b if sign > 0 else -b)
        if b is None:
            return a
        return a + b if sign > 0 else a - b

    for k in range(h // 2 + 1):
        ce, co, se, so = out[k]
        res[k] = (add(ce, co, 1), add(se, so, 1))
        if k != h - k:
            res[h - k] = (add(ce, co, -1), add(so, se, -1))
    return res


def masked(index, size, m):
    assert size == 4
    return (index, index + 1 - 2 * lax.rem(index, 2), lax.rem(index + 2, 4), 3 - index)[m]


def partners():
    nrow, ncol = lax.axis_size("row"), lax.axis_size("col")
    far = list(range(ncol // 2, ncol)) + list(range(ncol // 2))
    return [(p, q) for q in far for p in reversed(range(nrow))]


def seat(p, q):
    row = masked(lax.axis_index("row"), lax.axis_size("row"), p)
    col = masked(lax.axis_index("col"), lax.axis_size("col"), q)
    return row, col, row * lax.axis_size("col") + col


def deal(src_of, dst, send, recv, local):
    _, me, _ = place()
    copies = []
    own = pltpu.make_async_copy(src_of(me), dst, local)
    own.start()
    for i, (p, q) in enumerate(partners()):
        row, col, peer = seat(p, q)
        if p == 0 and q == 0:
            continue
        copy = pltpu.make_async_remote_copy(
            src_ref=src_of(peer), dst_ref=dst, send_sem=send.at[i], recv_sem=recv.at[i],
            device_id={"row": row, "col": col}, device_id_type=MESH,
        )
        copy.start()
        copies.append(copy)
    return copies + [own]


def start_shear(shear, xbuf, asend, arecv, loc):
    _, cols, rows, _ = xbuf.shape
    here = lax.axis_index("col")
    arrive = []
    for f in range(2):
        copies = []
        for q in list(range(cols // 2, cols)) + list(range(cols // 2)):
            other = masked(here, cols, q)
            src = shear.at[f, pl.ds(pl.multiple_of(other * rows, rows), rows), :]
            dst = xbuf.at[f, here]
            if q == 0:
                copy = pltpu.make_async_copy(src, dst, loc.at[f])
            else:
                copy = pltpu.make_async_remote_copy(
                    src_ref=src, dst_ref=dst, send_sem=asend.at[f, q], recv_sem=arecv.at[f, q],
                    device_id={"col": other}, device_id_type=MESH,
                )
            copy.start()
            copies.append(copy)
        arrive.append(copies)
    return arrive


def forward_y(arrive, xbuf, tables, tc, ts, out_ref, sbuf, bsend, brecv, loc):
    _, cols, rows, width = xbuf.shape
    per = width // LANES
    _, me, _ = place()
    base, first = ((high[...], low[...]) for high, low in tables)
    leave = []
    for f in range(2):
        for copy in arrive[f]:
            copy.wait()
        blocks = [xbuf[f, c, :, m * LANES : (m + 1) * LANES] for c in range(cols) for m in range(per)]
        sums = cos_sin_sums(blocks)
        h = len(blocks) // 2
        for k in range(h):
            if k == 0:
                both = jnp.concatenate([sums[0][0], sums[h][0]], axis=1)
                table = first
            else:
                re, im = sums[k][0], -sums[k][1]
                c, s = tc[k : k + 1, :], ts[k : k + 1, :]
                both = jnp.concatenate([re * c + im * s, im * c - re * s], axis=1)
                table = base
            got = mm(split_value(both), table)
            sbuf[2 * k, f] = got[:, :LANES]
            sbuf[2 * k + 1, f] = got[:, LANES:]
        leave += deal(
            lambda peer, f=f: sbuf.at[peer, f], out_ref.at[me, f], bsend.at[f], brecv.at[f], loc.at[f]
        )
    for copy in leave:
        copy.wait()


def turn(x, sign):
    return pltpu.roll(x, LANES // 2, 1) * sign


def middle(length, x_ref, smooth_ref, fwd, inv, tw_ref, out_ref, sbuf, send, recv, loc):
    fwd, inv = (fwd[0][...], fwd[1][...]), (inv[0][...], inv[1][...])
    radix = length // LANES
    h = radix // 2
    half = LANES // 2
    _, me, _ = place()
    lane = lax.broadcasted_iota(jnp.int32, (LANES, LANES), 1)
    row = lax.broadcasted_iota(jnp.int32, (LANES, LANES), 0)
    sign = jnp.where(lane < half, -1.0, 1.0)
    slot = me * half + lane % half
    block, spot = slot // LANES, slot % LANES
    freq = jnp.where(
        block == 0,
        jnp.where(spot < half, radix * spot, h + radix * (spot - half)),
        block + radix * spot,
    )
    packed = slot == 0
    ky = jnp.where(freq < length // 2, freq, freq - length).astype(jnp.float32)
    one = [x_ref[n, 0] for n in range(radix)]
    two_raw = [x_ref[n, 1] for n in range(radix)]
    alternate = jnp.where(row % 2 == 0, 1.0, -1.0)
    total = two_raw[0]
    for n in range(1, radix):
        total = total + two_raw[n]
    corner = jnp.sum(total * alternate, axis=0, keepdims=True)
    two = [jnp.where(packed, -sign * a, b) for a, b in zip(one, two_raw)]
    sums = (cos_sin_sums(one), cos_sin_sums(two))
    width = smooth_ref[0]
    scale = -2.0 * math.pi**2 * width * width
    edge = -float(length // 2)
    results = []
    for k in range(radix):
        j = min(k, radix - k)
        wc, ws = tw_ref[:, k : k + 1], tw_ref[:, radix + k : radix + k + 1]
        cols = []
        for f in range(2):
            c, s = sums[f][j]
            x = c
            if s is not None:
                x = c - turn(s, sign) if k == j else c + turn(s, sign)
            ix = turn(x, sign)
            if k:
                x, ix = wc * x - ws * ix, wc * ix + ws * x
            cols.append(jnp.concatenate([x, ix], axis=0))
        got = mm(fwd, split_value(jnp.concatenate(cols, axis=1)))
        g1, g2 = got[:, :LANES], got[:, LANES:]
        fx = k + radix * row
        kx = jnp.where(fx < length // 2, fx, fx - length).astype(jnp.float32)

        def kernel(ky):
            square = jnp.maximum(kx * kx + ky * ky, 1.0)
            damp = jnp.exp(scale * ((kx / length) ** 2 + (ky / length) ** 2))
            inverse = damp / square
            return (kx * kx - ky * ky) * inverse, -2.0 * kx * ky * inverse, damp

        kr, ki, _ = kernel(ky)
        nr, ni, damp_n = kernel(edge)
        last = fx == length // 2
        nr = jnp.where(last, 0.0, nr)
        ni_in = jnp.where(last, 0.0, ni)
        w1r = jnp.where(packed, 0.5 * (kr + nr), kr)
        w1i = jnp.where(packed, 0.5 * ni_in, jnp.where(last, ki, 0.0))
        w2r = jnp.where(packed, 0.5 * (kr - nr), jnp.where(last, 0.0, -ki))
        w2i = jnp.where(packed, -0.5 * ni_in, 0.0)
        z = w1r * g1 + w1i * turn(g1, sign) + w2r * g2 + w2i * turn(g2, sign)
        if k == 0:
            extra = jnp.where(packed & last & (lane >= half), -ni * corner, 0.0)
            z = z + extra
        iz = turn(z, sign)
        t = mm(inv, split_value(jnp.concatenate([z, iz], axis=0)))
        if k:
            t = wc * t + ws * turn(t, sign)
        results.append(t)
    sums = cos_sin_sums(results)
    for n in range(radix):
        j = min(n, radix - n)
        c, s = sums[j]
        x = c
        if s is not None:
            x = c + turn(s, sign) if n == j else c - turn(s, sign)
        sbuf[n] = x
    for copy in deal(lambda peer: sbuf.at[peer], out_ref.at[me], send, recv, loc.at[0]):
        copy.wait()


def inverse_y(z_ref, tables, tc, ts, out_ref, sq_ref, top_ref, bot_ref):
    count, rows, _ = z_ref.shape
    h = count // 2
    radix = count
    base, first = ((high[...], low[...]) for high, low in tables)
    real, imag = [None] * (h + 1), [None] * (h + 1)
    for k in range(h):
        both = jnp.concatenate([z_ref[2 * k], z_ref[2 * k + 1]], axis=1)
        got = mm(split_value(both), first if k == 0 else base)
        a, b = got[:, :LANES], got[:, LANES:]
        if k == 0:
            real[0], real[h] = a, b
        else:
            c, s = tc[k : k + 1, :], ts[k : k + 1, :]
            real[k], imag[k] = a * c - b * s, a * s + b * c
    square = None
    for n in range(h + 1):
        cosine, sine = real[0], None
        cosine = cosine + real[h] if n % 2 == 0 else cosine - real[h]
        for k in range(1, h):
            c, s = cs(k, n, radix)
            cosine = axpy(cosine, c, real[k])
            sine = axpy(sine, s, imag[k])
        for m in {n, (radix - n) % radix}:
            if sine is None:
                out = cosine
            else:
                out = cosine - sine if m == n else cosine + sine
            sl = slice(m * LANES, (m + 1) * LANES)
            out_ref[:, sl] = out
            top_ref[:, sl] = out[:1]
            bot_ref[:, sl] = out[rows - 1 :]
            sq = out * out
            square = sq if square is None else square + sq
    sq_ref[...] = jnp.sum(square, axis=0, keepdims=True)


def place():
    cols = lax.axis_size("col")
    count = lax.axis_size("row") * cols
    me = lax.axis_index("row") * cols + lax.axis_index("col")

    def at(d):
        peer = lax.rem(me + d, count)
        return {"row": peer // cols, "col": lax.rem(peer, cols)}

    return count, me, at


def greet(count, at):
    barrier = pltpu.get_barrier_semaphore()
    for d in range(1, count):
        pl.semaphore_signal(barrier, inc=1, device_id=at(d), device_id_type=MESH)
    pl.semaphore_wait(barrier, count - 1)


def spread(count, at, src, slots, send, recv):
    copies = []
    for d in range(1, count):
        copy = pltpu.make_async_remote_copy(
            src_ref=src, dst_ref=slots.at[d - 1], send_sem=send.at[d - 1],
            recv_sem=recv.at[d - 1], device_id=at(d), device_id_type=MESH,
        )
        copy.start()
        copies.append(copy)
    return copies


def gather_sum(copies, own, slots):
    for copy in copies:
        copy.wait()
    total = own[...]
    for d in range(slots.shape[0]):
        total = total + slots[d]
    return total


def peaks(pixels, x_ref, sq_ref, top_ref, bot_ref, off_ref, thr_ref, rms_ref, high_ref, cnt_ref,
          cnt_own, wide, above_ref, below_ref, slots, send, recv, hsend, hrecv):
    rows, width = x_ref.shape
    cells = width // CELL
    pad = 8
    count, _, at = place()
    copies = spread(count, at, sq_ref, slots.at[0], send.at[0], recv.at[0])
    edges = []
    for i, (src, dst, d) in enumerate(((bot_ref, above_ref, 1), (top_ref, below_ref, count - 1))):
        copy = pltpu.make_async_remote_copy(
            src_ref=src, dst_ref=dst, send_sem=hsend.at[i], recv_sem=hrecv.at[i],
            device_id=at(d), device_id_type=MESH,
        )
        copy.start()
        edges.append(copy)

    def three(x):
        side = jnp.maximum(pltpu.roll(x, 1, 1), pltpu.roll(x, width - 1, 1))
        return side, jnp.maximum(side, x)

    for p in range(rows // CELL):
        sl = slice(p * CELL, (p + 1) * CELL)
        wide[pad + p * CELL : pad + (p + 1) * CELL, :] = three(x_ref[sl, :])[1]
    same = lax.broadcasted_iota(jnp.int32, (cells, width), 1) // CELL == lax.broadcasted_iota(
        jnp.int32, (cells, width), 0
    )
    spread_table = same.astype(jnp.bfloat16)
    full = jnp.dot(
        off_ref[...].astype(jnp.bfloat16), spread_table, preferred_element_type=jnp.float32
    ).astype(jnp.int32)
    code = lax.broadcasted_iota(jnp.int32, (CELL, width), 0) * CELL + (
        lax.broadcasted_iota(jnp.int32, (CELL, width), 1) % CELL
    )
    tops, mids = [], []
    for copy in edges:
        copy.wait()
    wide[pad - 1 : pad, :] = three(jnp.broadcast_to(above_ref[...], (8, width)))[1][:1]
    wide[pad + rows : pad + rows + 1, :] = three(jnp.broadcast_to(below_ref[...], (8, width)))[1][:1]
    for p in range(rows // CELL):
        low = pad + p * CELL
        x = x_ref[p * CELL : (p + 1) * CELL, :]
        near = jnp.maximum(
            three(x)[0],
            jnp.maximum(wide[low - 1 : low - 1 + CELL, :], wide[low + 1 : low + 1 + CELL, :]),
        )
        chosen = full[p : p + 1, :] == code
        tops.append(jnp.sum(jnp.where(chosen, x - near, 0.0), axis=0, keepdims=True))
        mids.append(jnp.sum(jnp.where(chosen, x, 0.0), axis=0, keepdims=True))

    def gather(parts):
        dot = partial(
            lax.dot_general, dimension_numbers=(((1,), (1,)), ((), ())),
            preferred_element_type=jnp.float32,
        )
        x = jnp.concatenate(parts, axis=0)
        a = x.astype(jnp.bfloat16)
        rest = x - a.astype(jnp.float32)
        b = rest.astype(jnp.bfloat16)
        c = (rest - b.astype(jnp.float32)).astype(jnp.bfloat16)
        return dot(a, spread_table) + (dot(b, spread_table) + dot(c, spread_table))

    heights, values = gather(tops), gather(mids)
    square = gather_sum(copies, sq_ref, slots.at[0])
    rms = jnp.sqrt(jnp.sum(square, axis=1, keepdims=True) / pixels + 1e-06)
    rms_ref[...] = jnp.broadcast_to(rms, (1, LANES))
    heights, values = heights / rms, values / rms
    high_ref[...] = heights
    weight = 1.0 / (1.0 + jnp.exp(-heights / PEAK_SOFT))
    lane = lax.broadcasted_iota(jnp.int32, (1, LANES), 1)
    counts = jnp.zeros((1, LANES), jnp.float32)
    for k in range(thr_ref.shape[0]):
        level = BIN_STEP * thr_ref[k].astype(jnp.float32)
        above = weight / (1.0 + jnp.exp((level - values) / BIN_SOFT))
        one = jnp.sum(jnp.sum(above, axis=0, keepdims=True), axis=1, keepdims=True)
        counts = jnp.where(lane == k, one, counts)
    cnt_own[...] = counts
    copies = spread(count, at, cnt_own, slots.at[1], send.at[1], recv.at[1])
    cnt_ref[...] = gather_sum(copies, cnt_own, slots.at[1])


def kernel(sizes, shear, smooth_ref, off_hbm, thr_ref, wide_hbm, thin_hbm,
           x_ref, rms_ref, high_ref, cnt_ref,
           xbuf, sbuf, spec, field, zbuf, wide, off_ref, table, thin, sq_ref, cnt_own,
           top_ref, bot_ref, above_ref, below_ref, slots,
           asend, arecv, bsend, brecv, csend, crecv, esend, erecv, hsend, hrecv, loc):
    nx, ny = sizes
    count, _, at = place()
    extra = [
        pltpu.make_async_copy(src, dst, loc.at[i])
        for i, (src, dst) in enumerate(((wide_hbm, table), (thin_hbm, thin), (off_hbm, off_ref)))
    ]
    for copy in extra:
        copy.start()
    greet(count, at)
    arrive = start_shear(shear, xbuf, asend, arecv, loc.at[pl.ds(3, 2)])
    for copy in extra:
        copy.wait()
    full, part = 2 * LANES, LANES
    starts = [i * full for i in range(8)] + [8 * full + i * part for i in range(4)]
    sizes_of = [full] * 8 + [part] * 4
    t = [table.at[a : a + n] for a, n in zip(starts, sizes_of)]
    h = nx // LANES // 2
    tc, ts, tw = thin.at[0:h], thin.at[h : 2 * h], thin.at[2 * h : 2 * h + LANES]
    forward_y(arrive, xbuf, ((t[0], t[1]), (t[2], t[3])), tc, ts, spec, sbuf, bsend, brecv, loc.at[pl.ds(5, 2)])
    middle(nx, spec, smooth_ref, (t[8], t[9]), (t[10], t[11]), tw, zbuf, field, csend, crecv, loc.at[pl.ds(7, 1)])
    inverse_y(zbuf, ((t[4], t[5]), (t[6], t[7])), tc, ts, x_ref, sq_ref, top_ref, bot_ref)
    peaks(float(nx * ny), x_ref, sq_ref, top_ref, bot_ref, off_ref, thr_ref, rms_ref, high_ref, cnt_ref,
          cnt_own, wide, above_ref, below_ref, slots, esend, erecv, hsend, hrecv)


VM = pl.BlockSpec(memory_space=pltpu.VMEM)
HB = pl.BlockSpec(memory_space=pltpu.HBM)
SM = pl.BlockSpec(memory_space=pltpu.SMEM)
F32 = jnp.float32


def shape(*dims):
    return jax.ShapeDtypeStruct(dims, F32)


def one_map(shear, smoothing, offsets, thresholds):
    rows_in, cols_in = shear.shape[1:]
    nrow, ncol = lax.axis_size("row"), lax.axis_size("col")
    nx, ny = rows_in * nrow, cols_in * ncol
    count = nrow * ncol
    rows = nx // count
    base, first, inv, first_inv, tc, ts = y_tables(ny)
    fwd_x, inv_x, tw_x = x_tables(nx)
    parts = [half for t in (base, first, inv, first_inv, fwd_x, inv_x) for half in split_table(t)]
    table = jnp.concatenate(parts, axis=0)
    tw_x = np.pad(tw_x, ((0, 0), (0, LANES - tw_x.shape[1])))
    thin = jnp.asarray(np.concatenate([tc, ts, tw_x], axis=0).astype(np.float32))
    dma = pltpu.SemaphoreType.DMA
    vm = lambda *dims: pltpu.VMEM(dims, F32)
    kappa, rms, heights, counts = pl.pallas_call(
        partial(kernel, (nx, ny)),
        out_shape=(shape(rows, ny), shape(1, LANES), shape(*offsets.shape), shape(1, LANES)),
        in_specs=[HB, SM, HB, SM, HB, HB],
        out_specs=(VM, VM, VM, VM),
        scratch_shapes=[
            vm(2, ncol, rows, cols_in),
            vm(count, 2, rows, LANES),
            vm(count, 2, rows, LANES),
            vm(count, rows, LANES),
            vm(count, rows, LANES),
            vm(rows + 16, ny),
            pltpu.VMEM(offsets.shape, jnp.int32),
            pltpu.VMEM(table.shape, jnp.bfloat16),
            vm(*thin.shape),
            vm(1, LANES), vm(1, LANES),
            vm(1, ny), vm(1, ny), vm(1, ny), vm(1, ny),
            vm(2, count - 1, 1, LANES),
            dma((2, ncol)), dma((2, ncol)), dma((2, count)), dma((2, count)), dma((count,)), dma((count,)),
            dma((2, count - 1)), dma((2, count - 1)), dma((2,)), dma((2,)), dma((8,)),
        ],
        compiler_params=pltpu.CompilerParams(
            vmem_limit_bytes=48 * 2**20, collective_id=0, has_side_effects=True
        ),
    )(shear, smoothing, offsets, thresholds, table, thin)
    return kappa / rms[:, :1], heights, counts[0, : thresholds.shape[0]]


def body(shear, smoothing, offsets, thresholds):
    outs = [
        one_map(shear[:, m], smoothing[m : m + 1], offsets[m], thresholds[m])
        for m in range(shear.shape[1])
    ]
    return tuple(jnp.stack(parts) for parts in zip(*outs))


def solution(mesh):
    return jax.shard_map(
        body,
        mesh=mesh,
        in_specs=(
            P(None, "maps", "row", "col"),
            P("maps"),
            P("maps", GROUP, None),
            P("maps", None),
        ),
        out_specs=(P("maps", GROUP, None), P("maps", GROUP, None), P("maps", None)),
        check_vma=False,
    )
```

```python
from functools import partial
import math

import jax
import jax.numpy as jnp
import numpy as np
from jax import lax
from jax.experimental import pallas as pl
from jax.experimental.pallas import tpu as pltpu
from jax.sharding import PartitionSpec as P

LANES = 128
CELL = 16
MESH = pl.DeviceIdType.MESH
GROUP = ("row", "col")
PEAK_SOFT = 0.05
BIN_SOFT = 0.1
BIN_STEP = 0.25


def split_table(values):
    values = jnp.asarray(values.astype(np.float32))
    high = values.astype(jnp.bfloat16)
    low = (values - high.astype(jnp.float32)).astype(jnp.bfloat16)
    return high, low


def split_value(x):
    high = x.astype(jnp.bfloat16)
    return high, (x - high.astype(jnp.float32)).astype(jnp.bfloat16)


def mm(a, b):
    dot = partial(jnp.dot, preferred_element_type=jnp.float32)
    return dot(a[0], b[0]) + (dot(a[0], b[1]) + dot(a[1], b[0]))


def y_tables(length):
    radix = length // LANES
    half = LANES // 2
    i = np.arange(LANES)[:, None].astype(np.float64)
    l = np.arange(LANES)[None, :].astype(np.float64)
    th = 2 * np.pi * ((i * l) % LANES) / LANES
    c, s = np.cos(th), np.sin(th)

    def order(re, im):
        return np.concatenate([re[:, :half], im[:, :half], re[:, half:], im[:, half:]], axis=1)

    base = np.concatenate([order(c, -s), order(s, c)], axis=0)
    inv = np.concatenate([order(c, -s), order(s, c)], axis=0).T * 2.0 / length
    th0 = 2 * np.pi * ((i * l[:, :half]) % LANES) / LANES
    th8 = 2 * np.pi * ((i * (radix // 2 + radix * l[:, :half])) % length) / length
    zero = np.zeros_like(th0)
    im0 = -np.sin(th0)
    im0[:, 0] = (-1.0) ** np.arange(LANES)
    top = np.concatenate([np.cos(th0), im0, zero, zero], axis=1)
    bottom = np.concatenate([zero, zero, np.cos(th8), -np.sin(th8)], axis=1)
    first = np.concatenate([top, bottom], axis=0)
    first_inv = first.T * 2.0 / length
    first_inv[0] /= 2.0
    first_inv[half] /= 2.0
    k = np.arange(radix // 2)[:, None].astype(np.float64)
    tw = 2 * np.pi * k * np.arange(LANES)[None, :] / length
    return base, first, inv, first_inv, np.cos(tw), np.sin(tw)


def x_tables(length):
    radix = length // LANES
    i = np.arange(LANES)[:, None].astype(np.float64)
    th = 2 * np.pi * ((i * i.T) % LANES) / LANES
    fwd = np.concatenate([np.cos(th), -np.sin(th)], axis=1)
    inv = np.concatenate([np.cos(th), np.sin(th)], axis=1) / length
    tw = 2 * np.pi * i * np.arange(radix)[None, :] / length
    return fwd, inv, np.concatenate([np.cos(tw), np.sin(tw)], axis=1)


def cs(k, n, radix):
    a = (k * n) % radix
    c, s = math.cos(2 * math.pi * a / radix), math.sin(2 * math.pi * a / radix)
    return round(c, 15), round(s, 15)


def axpy(total, coef, x):
    if coef == 0.0:
        return total
    if coef == 1.0:
        return x if total is None else total + x
    if coef == -1.0:
        return -x if total is None else total - x
    return coef * x if total is None else total + coef * x


def cos_sin_sums(parts):
    radix = len(parts)
    h = radix // 2
    plus = [None] + [parts[n] + parts[radix - n] for n in range(1, h)]
    minus = [None] + [parts[n] - parts[radix - n] for n in range(1, h)]
    pe, po = parts[0] + parts[h], parts[0] - parts[h]
    out = []
    for k in range(h // 2 + 1):
        ce = pe if k % 2 == 0 else po
        co = None
        se = so = None
        for n in range(1, h):
            c, s = cs(k, n, radix)
            if n % 2 == 0:
                ce = axpy(ce, c, plus[n])
                se = axpy(se, s, minus[n])
            else:
                co = axpy(co, c, plus[n])
                so = axpy(so, s, minus[n])
        out.append((ce, co, se, so))
    res = [None] * (h + 1)

    def add(a, b, sign):
        if a is None:
            return None if b is None else (b if sign > 0 else -b)
        if b is None:
            return a
        return a + b if sign > 0 else a - b

    for k in range(h // 2 + 1):
        ce, co, se, so = out[k]
        res[k] = (add(ce, co, 1), add(se, so, 1))
        if k != h - k:
            res[h - k] = (add(ce, co, -1), add(so, se, -1))
    return res


def masked(index, size, m):
    assert size == 4
    return (index, index + 1 - 2 * lax.rem(index, 2), lax.rem(index + 2, 4), 3 - index)[m]


def partners():
    nrow, ncol = lax.axis_size("row"), lax.axis_size("col")
    far = list(range(ncol // 2, ncol)) + list(range(ncol // 2))
    return [(p, q) for q in far for p in reversed(range(nrow))]


def seat(p, q):
    row = masked(lax.axis_index("row"), lax.axis_size("row"), p)
    col = masked(lax.axis_index("col"), lax.axis_size("col"), q)
    return row, col, row * lax.axis_size("col") + col


def deal(src_of, dst, send, recv, local):
    _, me, _ = place()
    copies = []
    own = pltpu.make_async_copy(src_of(me), dst, local)
    own.start()
    for i, (p, q) in enumerate(partners()):
        row, col, peer = seat(p, q)
        if p == 0 and q == 0:
            continue
        copy = pltpu.make_async_remote_copy(
            src_ref=src_of(peer), dst_ref=dst, send_sem=send.at[i], recv_sem=recv.at[i],
            device_id={"row": row, "col": col}, device_id_type=MESH,
        )
        copy.start()
        copies.append(copy)
    return copies + [own]


def start_shear(shear, xbuf, asend, arecv, loc):
    _, cols, rows, _ = xbuf.shape
    here = lax.axis_index("col")
    arrive = []
    for f in range(2):
        copies = []
        for q in list(range(cols // 2, cols)) + list(range(cols // 2)):
            other = masked(here, cols, q)
            src = shear.at[f, pl.ds(pl.multiple_of(other * rows, rows), rows), :]
            dst = xbuf.at[f, here]
            if q == 0:
                copy = pltpu.make_async_copy(src, dst, loc.at[f])
            else:
                copy = pltpu.make_async_remote_copy(
                    src_ref=src, dst_ref=dst, send_sem=asend.at[f, q], recv_sem=arecv.at[f, q],
                    device_id={"col": other}, device_id_type=MESH,
                )
            copy.start()
            copies.append(copy)
        arrive.append(copies)
    return arrive


def forward_y(arrive, xbuf, tables, tc, ts, out_ref, sbuf, bsend, brecv, loc):
    _, cols, rows, width = xbuf.shape
    per = width // LANES
    _, me, _ = place()
    base, first = ((high[...], low[...]) for high, low in tables)
    leave = []
    for f in range(2):
        for copy in arrive[f]:
            copy.wait()
        blocks = [xbuf[f, c, :, m * LANES : (m + 1) * LANES] for c in range(cols) for m in range(per)]
        sums = cos_sin_sums(blocks)
        h = len(blocks) // 2
        for k in range(h):
            if k == 0:
                both = jnp.concatenate([sums[0][0], sums[h][0]], axis=1)
                table = first
            else:
                re, im = sums[k][0], -sums[k][1]
                c, s = tc[k : k + 1, :], ts[k : k + 1, :]
                both = jnp.concatenate([re * c + im * s, im * c - re * s], axis=1)
                table = base
            got = mm(split_value(both), table)
            sbuf[2 * k, f] = got[:, :LANES]
            sbuf[2 * k + 1, f] = got[:, LANES:]
        leave += deal(
            lambda peer, f=f: sbuf.at[peer, f], out_ref.at[me, f], bsend.at[f], brecv.at[f], loc.at[f]
        )
    return leave[: len(leave) // 2], leave[len(leave) // 2 :]


def turn(x, sign):
    return pltpu.roll(x, LANES // 2, 1) * sign


def middle(length, leave, gbuf, x_ref, smooth_ref, fwd, inv, tw_ref, out_ref, sbuf, send, recv, loc):
    fwd, inv = (fwd[0][...], fwd[1][...]), (inv[0][...], inv[1][...])
    radix = length // LANES
    h = radix // 2
    half = LANES // 2
    _, me, _ = place()
    lane = lax.broadcasted_iota(jnp.int32, (LANES, LANES), 1)
    row = lax.broadcasted_iota(jnp.int32, (LANES, LANES), 0)
    sign = jnp.where(lane < half, -1.0, 1.0)
    slot = me * half + lane % half
    block, spot = slot // LANES, slot % LANES
    freq = jnp.where(
        block == 0,
        jnp.where(spot < half, radix * spot, h + radix * (spot - half)),
        block + radix * spot,
    )
    packed = slot == 0
    ky = jnp.where(freq < length // 2, freq, freq - length).astype(jnp.float32)
    def spectra(k, sums):
        j = min(k, radix - k)
        c, s = sums[j]
        x = c
        if s is not None:
            x = c - turn(s, sign) if k == j else c + turn(s, sign)
        ix = turn(x, sign)
        if k:
            wc, ws = tw_ref[:, k : k + 1], tw_ref[:, radix + k : radix + k + 1]
            x, ix = wc * x - ws * ix, wc * ix + ws * x
        return jnp.concatenate([x, ix], axis=0)

    for copy in leave[0]:
        copy.wait()
    sums = cos_sin_sums([x_ref[n, 0] for n in range(radix)])
    for k in range(0, radix, 2):
        pair = jnp.concatenate([spectra(k, sums), spectra(k + 1, sums)], axis=1)
        got = mm(fwd, split_value(pair))
        gbuf[k] = got[:, :LANES]
        gbuf[k + 1] = got[:, LANES:]
    for copy in leave[1]:
        copy.wait()
    one = [x_ref[n, 0] for n in range(radix)]
    two_raw = [x_ref[n, 1] for n in range(radix)]
    alternate = jnp.where(row % 2 == 0, 1.0, -1.0)
    total = two_raw[0]
    for n in range(1, radix):
        total = total + two_raw[n]
    corner = jnp.sum(total * alternate, axis=0, keepdims=True)
    two = [jnp.where(packed, -sign * a, b) for a, b in zip(one, two_raw)]
    sums = cos_sin_sums(two)
    width = smooth_ref[0]
    scale = -2.0 * math.pi**2 * width * width
    edge = -float(length // 2)
    results = []
    for k in range(radix):
        wc, ws = tw_ref[:, k : k + 1], tw_ref[:, radix + k : radix + k + 1]
        if k % 2 == 0:
            pair = jnp.concatenate([spectra(k, sums), spectra(k + 1, sums)], axis=1)
            both = mm(fwd, split_value(pair))
        g1, g2 = gbuf[k], both[:, LANES * (k % 2) : LANES * (k % 2 + 1)]
        fx = k + radix * row
        kx = jnp.where(fx < length // 2, fx, fx - length).astype(jnp.float32)

        def kernel(ky):
            square = jnp.maximum(kx * kx + ky * ky, 1.0)
            damp = jnp.exp(scale * ((kx / length) ** 2 + (ky / length) ** 2))
            inverse = damp / square
            return (kx * kx - ky * ky) * inverse, -2.0 * kx * ky * inverse, damp

        kr, ki, _ = kernel(ky)
        nr, ni, damp_n = kernel(edge)
        last = fx == length // 2
        nr = jnp.where(last, 0.0, nr)
        ni_in = jnp.where(last, 0.0, ni)
        w1r = jnp.where(packed, 0.5 * (kr + nr), kr)
        w1i = jnp.where(packed, 0.5 * ni_in, jnp.where(last, ki, 0.0))
        w2r = jnp.where(packed, 0.5 * (kr - nr), jnp.where(last, 0.0, -ki))
        w2i = jnp.where(packed, -0.5 * ni_in, 0.0)
        z = w1r * g1 + w1i * turn(g1, sign) + w2r * g2 + w2i * turn(g2, sign)
        if k == 0:
            extra = jnp.where(packed & last & (lane >= half), -ni * corner, 0.0)
            z = z + extra
        iz = turn(z, sign)
        t = mm(inv, split_value(jnp.concatenate([z, iz], axis=0)))
        if k:
            t = wc * t + ws * turn(t, sign)
        results.append(t)
    sums = cos_sin_sums(results)
    for n in range(radix):
        j = min(n, radix - n)
        c, s = sums[j]
        x = c
        if s is not None:
            x = c + turn(s, sign) if n == j else c - turn(s, sign)
        sbuf[n] = x
    for copy in deal(lambda peer: sbuf.at[peer], out_ref.at[me], send, recv, loc.at[0]):
        copy.wait()


def inverse_y(z_ref, tables, tc, ts, out_ref, sq_ref, top_ref, bot_ref):
    count, rows, _ = z_ref.shape
    h = count // 2
    radix = count
    base, first = ((high[...], low[...]) for high, low in tables)
    real, imag = [None] * (h + 1), [None] * (h + 1)
    for k in range(h):
        both = jnp.concatenate([z_ref[2 * k], z_ref[2 * k + 1]], axis=1)
        got = mm(split_value(both), first if k == 0 else base)
        a, b = got[:, :LANES], got[:, LANES:]
        if k == 0:
            real[0], real[h] = a, b
        else:
            c, s = tc[k : k + 1, :], ts[k : k + 1, :]
            real[k], imag[k] = a * c - b * s, a * s + b * c
    square = None
    for n in range(h + 1):
        cosine, sine = real[0], None
        cosine = cosine + real[h] if n % 2 == 0 else cosine - real[h]
        for k in range(1, h):
            c, s = cs(k, n, radix)
            cosine = axpy(cosine, c, real[k])
            sine = axpy(sine, s, imag[k])
        for m in {n, (radix - n) % radix}:
            if sine is None:
                out = cosine
            else:
                out = cosine - sine if m == n else cosine + sine
            sl = slice(m * LANES, (m + 1) * LANES)
            out_ref[:, sl] = out
            top_ref[:, sl] = out[:1]
            bot_ref[:, sl] = out[rows - 1 :]
            sq = out * out
            square = sq if square is None else square + sq
    sq_ref[...] = jnp.sum(square, axis=0, keepdims=True)


def place():
    cols = lax.axis_size("col")
    count = lax.axis_size("row") * cols
    me = lax.axis_index("row") * cols + lax.axis_index("col")

    def at(d):
        peer = lax.rem(me + d, count)
        return {"row": peer // cols, "col": lax.rem(peer, cols)}

    return count, me, at


def greet(count, at):
    barrier = pltpu.get_barrier_semaphore()
    for d in range(1, count):
        pl.semaphore_signal(barrier, inc=1, device_id=at(d), device_id_type=MESH)
    pl.semaphore_wait(barrier, count - 1)


def spread(count, at, src, slots, send, recv):
    copies = []
    for d in range(1, count):
        copy = pltpu.make_async_remote_copy(
            src_ref=src, dst_ref=slots.at[d - 1], send_sem=send.at[d - 1],
            recv_sem=recv.at[d - 1], device_id=at(d), device_id_type=MESH,
        )
        copy.start()
        copies.append(copy)
    return copies


def gather_sum(copies, own, slots):
    for copy in copies:
        copy.wait()
    total = own[...]
    for d in range(slots.shape[0]):
        total = total + slots[d]
    return total


def peaks(pixels, x_ref, sq_ref, top_ref, bot_ref, off_ref, thr_ref, rms_ref, high_ref, cnt_ref,
          cnt_own, wide, above_ref, below_ref, slots, send, recv, hsend, hrecv):
    rows, width = x_ref.shape
    cells = width // CELL
    pad = 8
    count, _, at = place()
    copies = spread(count, at, sq_ref, slots.at[0], send.at[0], recv.at[0])
    edges = []
    for i, (src, dst, d) in enumerate(((bot_ref, above_ref, 1), (top_ref, below_ref, count - 1))):
        copy = pltpu.make_async_remote_copy(
            src_ref=src, dst_ref=dst, send_sem=hsend.at[i], recv_sem=hrecv.at[i],
            device_id=at(d), device_id_type=MESH,
        )
        copy.start()
        edges.append(copy)

    def three(x):
        side = jnp.maximum(pltpu.roll(x, 1, 1), pltpu.roll(x, width - 1, 1))
        return side, jnp.maximum(side, x)

    for p in range(rows // CELL):
        sl = slice(p * CELL, (p + 1) * CELL)
        wide[pad + p * CELL : pad + (p + 1) * CELL, :] = three(x_ref[sl, :])[1]
    same = lax.broadcasted_iota(jnp.int32, (cells, width), 1) // CELL == lax.broadcasted_iota(
        jnp.int32, (cells, width), 0
    )
    spread_table = same.astype(jnp.bfloat16)
    full = jnp.dot(
        off_ref[...].astype(jnp.bfloat16), spread_table, preferred_element_type=jnp.float32
    ).astype(jnp.int32)
    code = lax.broadcasted_iota(jnp.int32, (CELL, width), 0) * CELL + (
        lax.broadcasted_iota(jnp.int32, (CELL, width), 1) % CELL
    )
    tops, mids = [], []
    for copy in edges:
        copy.wait()
    wide[pad - 1 : pad, :] = three(jnp.broadcast_to(above_ref[...], (8, width)))[1][:1]
    wide[pad + rows : pad + rows + 1, :] = three(jnp.broadcast_to(below_ref[...], (8, width)))[1][:1]
    for p in range(rows // CELL):
        low = pad + p * CELL
        x = x_ref[p * CELL : (p + 1) * CELL, :]
        near = jnp.maximum(
            three(x)[0],
            jnp.maximum(wide[low - 1 : low - 1 + CELL, :], wide[low + 1 : low + 1 + CELL, :]),
        )
        chosen = full[p : p + 1, :] == code
        tops.append(jnp.sum(jnp.where(chosen, x - near, 0.0), axis=0, keepdims=True))
        mids.append(jnp.sum(jnp.where(chosen, x, 0.0), axis=0, keepdims=True))

    def gather(parts):
        dot = partial(
            lax.dot_general, dimension_numbers=(((1,), (1,)), ((), ())),
            preferred_element_type=jnp.float32,
        )
        x = jnp.concatenate(parts, axis=0)
        a = x.astype(jnp.bfloat16)
        rest = x - a.astype(jnp.float32)
        b = rest.astype(jnp.bfloat16)
        c = (rest - b.astype(jnp.float32)).astype(jnp.bfloat16)
        return dot(a, spread_table) + (dot(b, spread_table) + dot(c, spread_table))

    heights, values = gather(tops), gather(mids)
    square = gather_sum(copies, sq_ref, slots.at[0])
    rms = jnp.sqrt(jnp.sum(square, axis=1, keepdims=True) / pixels + 1e-06)
    rms_ref[...] = jnp.broadcast_to(rms, (1, LANES))
    heights, values = heights / rms, values / rms
    high_ref[...] = heights
    weight = 1.0 / (1.0 + jnp.exp(-heights / PEAK_SOFT))
    lane = lax.broadcasted_iota(jnp.int32, (1, LANES), 1)
    counts = jnp.zeros((1, LANES), jnp.float32)
    for k in range(thr_ref.shape[0]):
        level = BIN_STEP * thr_ref[k].astype(jnp.float32)
        above = weight / (1.0 + jnp.exp((level - values) / BIN_SOFT))
        one = jnp.sum(jnp.sum(above, axis=0, keepdims=True), axis=1, keepdims=True)
        counts = jnp.where(lane == k, one, counts)
    cnt_own[...] = counts
    copies = spread(count, at, cnt_own, slots.at[1], send.at[1], recv.at[1])
    cnt_ref[...] = gather_sum(copies, cnt_own, slots.at[1])


def kernel(sizes, shear, smooth_ref, off_hbm, thr_ref, wide_hbm, thin_hbm,
           x_ref, rms_ref, high_ref, cnt_ref,
           xbuf, sbuf, spec, gbuf, field, zbuf, wide, off_ref, table, thin, sq_ref, cnt_own,
           top_ref, bot_ref, above_ref, below_ref, slots,
           asend, arecv, bsend, brecv, csend, crecv, esend, erecv, hsend, hrecv, loc):
    nx, ny = sizes
    count, _, at = place()
    extra = [
        pltpu.make_async_copy(src, dst, loc.at[i])
        for i, (src, dst) in enumerate(((wide_hbm, table), (thin_hbm, thin), (off_hbm, off_ref)))
    ]
    for copy in extra:
        copy.start()
    greet(count, at)
    arrive = start_shear(shear, xbuf, asend, arecv, loc.at[pl.ds(3, 2)])
    for copy in extra:
        copy.wait()
    full, part = 2 * LANES, LANES
    starts = [i * full for i in range(8)] + [8 * full + i * part for i in range(4)]
    sizes_of = [full] * 8 + [part] * 4
    t = [table.at[a : a + n] for a, n in zip(starts, sizes_of)]
    h = nx // LANES // 2
    tc, ts, tw = thin.at[0:h], thin.at[h : 2 * h], thin.at[2 * h : 2 * h + LANES]
    leave = forward_y(arrive, xbuf, ((t[0], t[1]), (t[2], t[3])), tc, ts, spec, sbuf, bsend, brecv, loc.at[pl.ds(5, 2)])
    middle(nx, leave, gbuf, spec, smooth_ref, (t[8], t[9]), (t[10], t[11]), tw, zbuf, field, csend, crecv, loc.at[pl.ds(7, 1)])
    inverse_y(zbuf, ((t[4], t[5]), (t[6], t[7])), tc, ts, x_ref, sq_ref, top_ref, bot_ref)
    peaks(float(nx * ny), x_ref, sq_ref, top_ref, bot_ref, off_ref, thr_ref, rms_ref, high_ref, cnt_ref,
          cnt_own, wide, above_ref, below_ref, slots, esend, erecv, hsend, hrecv)


VM = pl.BlockSpec(memory_space=pltpu.VMEM)
HB = pl.BlockSpec(memory_space=pltpu.HBM)
SM = pl.BlockSpec(memory_space=pltpu.SMEM)
F32 = jnp.float32


def shape(*dims):
    return jax.ShapeDtypeStruct(dims, F32)


def one_map(shear, smoothing, offsets, thresholds):
    rows_in, cols_in = shear.shape[1:]
    nrow, ncol = lax.axis_size("row"), lax.axis_size("col")
    nx, ny = rows_in * nrow, cols_in * ncol
    count = nrow * ncol
    rows = nx // count
    base, first, inv, first_inv, tc, ts = y_tables(ny)
    fwd_x, inv_x, tw_x = x_tables(nx)
    parts = [half for t in (base, first, inv, first_inv, fwd_x, inv_x) for half in split_table(t)]
    table = jnp.concatenate(parts, axis=0)
    tw_x = np.pad(tw_x, ((0, 0), (0, LANES - tw_x.shape[1])))
    thin = jnp.asarray(np.concatenate([tc, ts, tw_x], axis=0).astype(np.float32))
    dma = pltpu.SemaphoreType.DMA
    vm = lambda *dims: pltpu.VMEM(dims, F32)
    kappa, rms, heights, counts = pl.pallas_call(
        partial(kernel, (nx, ny)),
        out_shape=(shape(rows, ny), shape(1, LANES), shape(*offsets.shape), shape(1, LANES)),
        in_specs=[HB, SM, HB, SM, HB, HB],
        out_specs=(VM, VM, VM, VM),
        scratch_shapes=[
            vm(2, ncol, rows, cols_in),
            vm(count, 2, rows, LANES),
            vm(count, 2, rows, LANES),
            vm(nx // LANES, LANES, LANES),
            vm(count, rows, LANES),
            vm(count, rows, LANES),
            vm(rows + 16, ny),
            pltpu.VMEM(offsets.shape, jnp.int32),
            pltpu.VMEM(table.shape, jnp.bfloat16),
            vm(*thin.shape),
            vm(1, LANES), vm(1, LANES),
            vm(1, ny), vm(1, ny), vm(1, ny), vm(1, ny),
            vm(2, count - 1, 1, LANES),
            dma((2, ncol)), dma((2, ncol)), dma((2, count)), dma((2, count)), dma((count,)), dma((count,)),
            dma((2, count - 1)), dma((2, count - 1)), dma((2,)), dma((2,)), dma((8,)),
        ],
        compiler_params=pltpu.CompilerParams(
            vmem_limit_bytes=63 * 2**20, collective_id=0, has_side_effects=True
        ),
    )(shear, smoothing, offsets, thresholds, table, thin)
    return kappa / rms[:, :1], heights, counts[0, : thresholds.shape[0]]


def body(shear, smoothing, offsets, thresholds):
    outs = [
        one_map(shear[:, m], smoothing[m : m + 1], offsets[m], thresholds[m])
        for m in range(shear.shape[1])
    ]
    return tuple(jnp.stack(parts) for parts in zip(*outs))


def solution(mesh):
    return jax.shard_map(
        body,
        mesh=mesh,
        in_specs=(
            P(None, "maps", "row", "col"),
            P("maps"),
            P("maps", GROUP, None),
            P("maps", None),
        ),
        out_specs=(P("maps", GROUP, None), P("maps", GROUP, None), P("maps", None)),
        check_vma=False,
    )
```

```python
from functools import partial
import math

import jax
import jax.numpy as jnp
import numpy as np
from jax import lax
from jax.experimental import pallas as pl
from jax.experimental.pallas import tpu as pltpu
from jax.sharding import PartitionSpec as P

LANES = 128
CELL = 16
MESH = pl.DeviceIdType.MESH
GROUP = ("row", "col")
PEAK_SOFT = 0.05
BIN_SOFT = 0.1
BIN_STEP = 0.25


def split_table(values):
    values = jnp.asarray(values.astype(np.float32))
    high = values.astype(jnp.bfloat16)
    low = (values - high.astype(jnp.float32)).astype(jnp.bfloat16)
    return high, low


def split_value(x):
    high = x.astype(jnp.bfloat16)
    return high, (x - high.astype(jnp.float32)).astype(jnp.bfloat16)


def mm(a, b):
    dot = partial(jnp.dot, preferred_element_type=jnp.float32)
    return dot(a[0], b[0]) + (dot(a[0], b[1]) + dot(a[1], b[0]))


def y_tables(length):
    radix = length // LANES
    half = LANES // 2
    i = np.arange(LANES)[:, None].astype(np.float64)
    l = np.arange(LANES)[None, :].astype(np.float64)
    th = 2 * np.pi * ((i * l) % LANES) / LANES
    c, s = np.cos(th), np.sin(th)

    def order(re, im):
        return np.concatenate([re[:, :half], im[:, :half], re[:, half:], im[:, half:]], axis=1)

    base = np.concatenate([order(c, -s), order(s, c)], axis=0)
    inv = np.concatenate([order(c, -s), order(s, c)], axis=0).T * 2.0 / length
    th0 = 2 * np.pi * ((i * l[:, :half]) % LANES) / LANES
    th8 = 2 * np.pi * ((i * (radix // 2 + radix * l[:, :half])) % length) / length
    zero = np.zeros_like(th0)
    im0 = -np.sin(th0)
    im0[:, 0] = (-1.0) ** np.arange(LANES)
    top = np.concatenate([np.cos(th0), im0, zero, zero], axis=1)
    bottom = np.concatenate([zero, zero, np.cos(th8), -np.sin(th8)], axis=1)
    first = np.concatenate([top, bottom], axis=0)
    first_inv = first.T * 2.0 / length
    first_inv[0] /= 2.0
    first_inv[half] /= 2.0
    k = np.arange(radix // 2)[:, None].astype(np.float64)
    tw = 2 * np.pi * k * np.arange(LANES)[None, :] / length
    return base, first, inv, first_inv, np.cos(tw), np.sin(tw)


def x_tables(length):
    radix = length // LANES
    i = np.arange(LANES)[:, None].astype(np.float64)
    th = 2 * np.pi * ((i * i.T) % LANES) / LANES
    fwd = np.concatenate([np.cos(th), -np.sin(th)], axis=1)
    inv = np.concatenate([np.cos(th), np.sin(th)], axis=1) / length
    tw = 2 * np.pi * i * np.arange(radix)[None, :] / length
    return fwd, inv, np.concatenate([np.cos(tw), np.sin(tw)], axis=1)


def cs(k, n, radix):
    a = (k * n) % radix
    c, s = math.cos(2 * math.pi * a / radix), math.sin(2 * math.pi * a / radix)
    return round(c, 15), round(s, 15)


def axpy(total, coef, x):
    if coef == 0.0:
        return total
    if coef == 1.0:
        return x if total is None else total + x
    if coef == -1.0:
        return -x if total is None else total - x
    return coef * x if total is None else total + coef * x


def cos_sin_sums(parts):
    radix = len(parts)
    h = radix // 2
    plus = [None] + [parts[n] + parts[radix - n] for n in range(1, h)]
    minus = [None] + [parts[n] - parts[radix - n] for n in range(1, h)]
    pe, po = parts[0] + parts[h], parts[0] - parts[h]
    out = []
    for k in range(h // 2 + 1):
        ce = pe if k % 2 == 0 else po
        co = None
        se = so = None
        for n in range(1, h):
            c, s = cs(k, n, radix)
            if n % 2 == 0:
                ce = axpy(ce, c, plus[n])
                se = axpy(se, s, minus[n])
            else:
                co = axpy(co, c, plus[n])
                so = axpy(so, s, minus[n])
        out.append((ce, co, se, so))
    res = [None] * (h + 1)

    def add(a, b, sign):
        if a is None:
            return None if b is None else (b if sign > 0 else -b)
        if b is None:
            return a
        return a + b if sign > 0 else a - b

    for k in range(h // 2 + 1):
        ce, co, se, so = out[k]
        res[k] = (add(ce, co, 1), add(se, so, 1))
        if k != h - k:
            res[h - k] = (add(ce, co, -1), add(so, se, -1))
    return res


def masked(index, size, m):
    assert size == 4
    return (index, index + 1 - 2 * lax.rem(index, 2), lax.rem(index + 2, 4), 3 - index)[m]


def partners():
    nrow, ncol = lax.axis_size("row"), lax.axis_size("col")
    far = list(range(ncol // 2, ncol)) + list(range(ncol // 2))
    return [(p, q) for q in far for p in reversed(range(nrow))]


def seat(p, q):
    row = masked(lax.axis_index("row"), lax.axis_size("row"), p)
    col = masked(lax.axis_index("col"), lax.axis_size("col"), q)
    return row, col, row * lax.axis_size("col") + col


def deal(src_of, dst, send, recv, local):
    _, me, _ = place()
    copies = []
    own = pltpu.make_async_copy(src_of(me), dst, local)
    own.start()
    for i, (p, q) in enumerate(partners()):
        row, col, peer = seat(p, q)
        if p == 0 and q == 0:
            continue
        copy = pltpu.make_async_remote_copy(
            src_ref=src_of(peer), dst_ref=dst, send_sem=send.at[i], recv_sem=recv.at[i],
            device_id={"row": row, "col": col}, device_id_type=MESH,
        )
        copy.start()
        copies.append(copy)
    return copies + [own]


def start_shear(shear, xbuf, asend, arecv, loc):
    _, cols, rows, _ = xbuf.shape
    here = lax.axis_index("col")
    arrive = []
    for f in range(2):
        copies = []
        for q in list(range(cols // 2, cols)) + list(range(cols // 2)):
            other = masked(here, cols, q)
            src = shear.at[f, pl.ds(pl.multiple_of(other * rows, rows), rows), :]
            dst = xbuf.at[f, here]
            if q == 0:
                copy = pltpu.make_async_copy(src, dst, loc.at[f])
            else:
                copy = pltpu.make_async_remote_copy(
                    src_ref=src, dst_ref=dst, send_sem=asend.at[f, q], recv_sem=arecv.at[f, q],
                    device_id={"col": other}, device_id_type=MESH,
                )
            copy.start()
            copies.append(copy)
        arrive.append(copies)
    return arrive


def forward_y(arrive, xbuf, tables, tc, ts, out_ref, sbuf, bsend, brecv, loc):
    _, cols, rows, width = xbuf.shape
    per = width // LANES
    _, me, _ = place()
    base, first = ((high[...], low[...]) for high, low in tables)
    leave = []
    for f in range(2):
        for copy in arrive[f]:
            copy.wait()
        blocks = [xbuf[f, c, :, m * LANES : (m + 1) * LANES] for c in range(cols) for m in range(per)]
        sums = cos_sin_sums(blocks)
        h = len(blocks) // 2
        for k in range(h):
            if k == 0:
                both = jnp.concatenate([sums[0][0], sums[h][0]], axis=1)
                table = first
            else:
                re, im = sums[k][0], -sums[k][1]
                c, s = tc[k : k + 1, :], ts[k : k + 1, :]
                both = jnp.concatenate([re * c + im * s, im * c - re * s], axis=1)
                table = base
            got = mm(split_value(both), table)
            sbuf[2 * k, f] = got[:, :LANES]
            sbuf[2 * k + 1, f] = got[:, LANES:]
        leave += deal(
            lambda peer, f=f: sbuf.at[peer, f], out_ref.at[me, f], bsend.at[f], brecv.at[f], loc.at[f]
        )
    return leave[: len(leave) // 2], leave[len(leave) // 2 :]


def turn(x, sign):
    return pltpu.roll(x, LANES // 2, 1) * sign


def middle(length, leave, gbuf, wbuf, x_ref, smooth_ref, fwd, inv, tw_ref, out_ref, sbuf, send, recv, loc):
    fwd, inv = (fwd[0][...], fwd[1][...]), (inv[0][...], inv[1][...])
    radix = length // LANES
    h = radix // 2
    half = LANES // 2
    _, me, _ = place()
    lane = lax.broadcasted_iota(jnp.int32, (LANES, LANES), 1)
    row = lax.broadcasted_iota(jnp.int32, (LANES, LANES), 0)
    sign = jnp.where(lane < half, -1.0, 1.0)
    slot = me * half + lane % half
    block, spot = slot // LANES, slot % LANES
    freq = jnp.where(
        block == 0,
        jnp.where(spot < half, radix * spot, h + radix * (spot - half)),
        block + radix * spot,
    )
    packed = slot == 0
    ky = jnp.where(freq < length // 2, freq, freq - length).astype(jnp.float32)
    def spectra(k, sums):
        j = min(k, radix - k)
        c, s = sums[j]
        x = c
        if s is not None:
            x = c - turn(s, sign) if k == j else c + turn(s, sign)
        ix = turn(x, sign)
        if k:
            wc, ws = tw_ref[:, k : k + 1], tw_ref[:, radix + k : radix + k + 1]
            x, ix = wc * x - ws * ix, wc * ix + ws * x
        return jnp.concatenate([x, ix], axis=0)

    width = smooth_ref[0]
    scale = -2.0 * math.pi**2 * width * width
    edge = -float(length // 2)

    def weigh(k, g1):
        fx = k + radix * row
        kx = jnp.where(fx < length // 2, fx, fx - length).astype(jnp.float32)

        def kernel(ky):
            square = jnp.maximum(kx * kx + ky * ky, 1.0)
            damp = jnp.exp(scale * ((kx / length) ** 2 + (ky / length) ** 2))
            inverse = damp / square
            return (kx * kx - ky * ky) * inverse, -2.0 * kx * ky * inverse, damp

        kr, ki, _ = kernel(ky)
        nr, ni, damp_n = kernel(edge)
        last = fx == length // 2
        nr = jnp.where(last, 0.0, nr)
        ni_in = jnp.where(last, 0.0, ni)
        w1r = jnp.where(packed, 0.5 * (kr + nr), kr)
        w1i = jnp.where(packed, 0.5 * ni_in, jnp.where(last, ki, 0.0))
        w2r = jnp.where(packed, 0.5 * (kr - nr), jnp.where(last, 0.0, -ki))
        w2i = jnp.where(packed, -0.5 * ni_in, 0.0)
        gbuf[k] = w1r * g1 + w1i * turn(g1, sign)
        wbuf[k, 0] = w2r
        wbuf[k, 1] = w2i
        if k == 0:
            wbuf[radix, 0] = jnp.where(packed & last & (lane >= half), -ni, 0.0)

    for copy in leave[0]:
        copy.wait()
    sums = cos_sin_sums([x_ref[n, 0] for n in range(radix)])
    for k in range(0, radix, 2):
        pair = jnp.concatenate([spectra(k, sums), spectra(k + 1, sums)], axis=1)
        got = mm(fwd, split_value(pair))
        weigh(k, got[:, :LANES])
        weigh(k + 1, got[:, LANES:])
    for copy in leave[1]:
        copy.wait()
    one = [x_ref[n, 0] for n in range(radix)]
    two_raw = [x_ref[n, 1] for n in range(radix)]
    alternate = jnp.where(row % 2 == 0, 1.0, -1.0)
    total = two_raw[0]
    for n in range(1, radix):
        total = total + two_raw[n]
    corner = jnp.sum(total * alternate, axis=0, keepdims=True)
    two = [jnp.where(packed, -sign * a, b) for a, b in zip(one, two_raw)]
    sums = cos_sin_sums(two)
    results = []
    for k in range(radix):
        wc, ws = tw_ref[:, k : k + 1], tw_ref[:, radix + k : radix + k + 1]
        if k % 2 == 0:
            pair = jnp.concatenate([spectra(k, sums), spectra(k + 1, sums)], axis=1)
            both = mm(fwd, split_value(pair))
        g2 = both[:, LANES * (k % 2) : LANES * (k % 2 + 1)]
        z = gbuf[k] + wbuf[k, 0] * g2 + wbuf[k, 1] * turn(g2, sign)
        if k == 0:
            z = z + wbuf[radix, 0] * corner
        iz = turn(z, sign)
        t = mm(inv, split_value(jnp.concatenate([z, iz], axis=0)))
        if k:
            t = wc * t + ws * turn(t, sign)
        results.append(t)
    sums = cos_sin_sums(results)
    for n in range(radix):
        j = min(n, radix - n)
        c, s = sums[j]
        x = c
        if s is not None:
            x = c + turn(s, sign) if n == j else c - turn(s, sign)
        sbuf[n] = x
    for copy in deal(lambda peer: sbuf.at[peer], out_ref.at[me], send, recv, loc.at[0]):
        copy.wait()


def inverse_y(z_ref, tables, tc, ts, out_ref, sq_ref, top_ref, bot_ref):
    count, rows, _ = z_ref.shape
    h = count // 2
    radix = count
    base, first = ((high[...], low[...]) for high, low in tables)
    real, imag = [None] * (h + 1), [None] * (h + 1)
    for k in range(h):
        both = jnp.concatenate([z_ref[2 * k], z_ref[2 * k + 1]], axis=1)
        got = mm(split_value(both), first if k == 0 else base)
        a, b = got[:, :LANES], got[:, LANES:]
        if k == 0:
            real[0], real[h] = a, b
        else:
            c, s = tc[k : k + 1, :], ts[k : k + 1, :]
            real[k], imag[k] = a * c - b * s, a * s + b * c
    square = None
    for n in range(h + 1):
        cosine, sine = real[0], None
        cosine = cosine + real[h] if n % 2 == 0 else cosine - real[h]
        for k in range(1, h):
            c, s = cs(k, n, radix)
            cosine = axpy(cosine, c, real[k])
            sine = axpy(sine, s, imag[k])
        for m in {n, (radix - n) % radix}:
            if sine is None:
                out = cosine
            else:
                out = cosine - sine if m == n else cosine + sine
            sl = slice(m * LANES, (m + 1) * LANES)
            out_ref[:, sl] = out
            top_ref[:, sl] = out[:1]
            bot_ref[:, sl] = out[rows - 1 :]
            sq = out * out
            square = sq if square is None else square + sq
    sq_ref[...] = jnp.sum(square, axis=0, keepdims=True)


def place():
    cols = lax.axis_size("col")
    count = lax.axis_size("row") * cols
    me = lax.axis_index("row") * cols + lax.axis_index("col")

    def at(d):
        peer = lax.rem(me + d, count)
        return {"row": peer // cols, "col": lax.rem(peer, cols)}

    return count, me, at


def greet(count, at):
    barrier = pltpu.get_barrier_semaphore()
    for d in range(1, count):
        pl.semaphore_signal(barrier, inc=1, device_id=at(d), device_id_type=MESH)
    pl.semaphore_wait(barrier, count - 1)


def spread(count, at, src, slots, send, recv):
    copies = []
    for d in range(1, count):
        copy = pltpu.make_async_remote_copy(
            src_ref=src, dst_ref=slots.at[d - 1], send_sem=send.at[d - 1],
            recv_sem=recv.at[d - 1], device_id=at(d), device_id_type=MESH,
        )
        copy.start()
        copies.append(copy)
    return copies


def gather_sum(copies, own, slots):
    for copy in copies:
        copy.wait()
    total = own[...]
    for d in range(slots.shape[0]):
        total = total + slots[d]
    return total


def peaks(pixels, x_ref, sq_ref, top_ref, bot_ref, off_ref, thr_ref, rms_ref, high_ref, cnt_ref,
          cnt_own, wide, above_ref, below_ref, slots, send, recv, hsend, hrecv):
    rows, width = x_ref.shape
    cells = width // CELL
    pad = 8
    count, _, at = place()
    copies = spread(count, at, sq_ref, slots.at[0], send.at[0], recv.at[0])
    edges = []
    for i, (src, dst, d) in enumerate(((bot_ref, above_ref, 1), (top_ref, below_ref, count - 1))):
        copy = pltpu.make_async_remote_copy(
            src_ref=src, dst_ref=dst, send_sem=hsend.at[i], recv_sem=hrecv.at[i],
            device_id=at(d), device_id_type=MESH,
        )
        copy.start()
        edges.append(copy)

    def three(x):
        side = jnp.maximum(pltpu.roll(x, 1, 1), pltpu.roll(x, width - 1, 1))
        return side, jnp.maximum(side, x)

    for p in range(rows // CELL):
        sl = slice(p * CELL, (p + 1) * CELL)
        wide[pad + p * CELL : pad + (p + 1) * CELL, :] = three(x_ref[sl, :])[1]
    same = lax.broadcasted_iota(jnp.int32, (cells, width), 1) // CELL == lax.broadcasted_iota(
        jnp.int32, (cells, width), 0
    )
    spread_table = same.astype(jnp.bfloat16)
    full = jnp.dot(
        off_ref[...].astype(jnp.bfloat16), spread_table, preferred_element_type=jnp.float32
    ).astype(jnp.int32)
    code = lax.broadcasted_iota(jnp.int32, (CELL, width), 0) * CELL + (
        lax.broadcasted_iota(jnp.int32, (CELL, width), 1) % CELL
    )
    tops, mids = [], []
    for copy in edges:
        copy.wait()
    wide[pad - 1 : pad, :] = three(jnp.broadcast_to(above_ref[...], (8, width)))[1][:1]
    wide[pad + rows : pad + rows + 1, :] = three(jnp.broadcast_to(below_ref[...], (8, width)))[1][:1]
    for p in range(rows // CELL):
        low = pad + p * CELL
        x = x_ref[p * CELL : (p + 1) * CELL, :]
        near = jnp.maximum(
            three(x)[0],
            jnp.maximum(wide[low - 1 : low - 1 + CELL, :], wide[low + 1 : low + 1 + CELL, :]),
        )
        chosen = full[p : p + 1, :] == code
        tops.append(jnp.sum(jnp.where(chosen, x - near, 0.0), axis=0, keepdims=True))
        mids.append(jnp.sum(jnp.where(chosen, x, 0.0), axis=0, keepdims=True))

    def gather(parts):
        dot = partial(
            lax.dot_general, dimension_numbers=(((1,), (1,)), ((), ())),
            preferred_element_type=jnp.float32,
        )
        x = jnp.concatenate(parts, axis=0)
        a = x.astype(jnp.bfloat16)
        rest = x - a.astype(jnp.float32)
        b = rest.astype(jnp.bfloat16)
        c = (rest - b.astype(jnp.float32)).astype(jnp.bfloat16)
        return dot(a, spread_table) + (dot(b, spread_table) + dot(c, spread_table))

    heights, values = gather(tops), gather(mids)
    square = gather_sum(copies, sq_ref, slots.at[0])
    rms = jnp.sqrt(jnp.sum(square, axis=1, keepdims=True) / pixels + 1e-06)
    rms_ref[...] = jnp.broadcast_to(rms, (1, LANES))
    heights, values = heights / rms, values / rms
    high_ref[...] = heights
    weight = 1.0 / (1.0 + jnp.exp(-heights / PEAK_SOFT))
    lane = lax.broadcasted_iota(jnp.int32, (1, LANES), 1)
    counts = jnp.zeros((1, LANES), jnp.float32)
    for k in range(thr_ref.shape[0]):
        level = BIN_STEP * thr_ref[k].astype(jnp.float32)
        above = weight / (1.0 + jnp.exp((level - values) / BIN_SOFT))
        one = jnp.sum(jnp.sum(above, axis=0, keepdims=True), axis=1, keepdims=True)
        counts = jnp.where(lane == k, one, counts)
    cnt_own[...] = counts
    copies = spread(count, at, cnt_own, slots.at[1], send.at[1], recv.at[1])
    cnt_ref[...] = gather_sum(copies, cnt_own, slots.at[1])


def kernel(sizes, shear, smooth_ref, off_hbm, thr_ref, wide_hbm, thin_hbm,
           x_ref, rms_ref, high_ref, cnt_ref,
           xbuf, sbuf, spec, gbuf, wbuf, field, zbuf, wide, off_ref, table, thin, sq_ref, cnt_own,
           top_ref, bot_ref, above_ref, below_ref, slots,
           asend, arecv, bsend, brecv, csend, crecv, esend, erecv, hsend, hrecv, loc):
    nx, ny = sizes
    count, _, at = place()
    extra = [
        pltpu.make_async_copy(src, dst, loc.at[i])
        for i, (src, dst) in enumerate(((wide_hbm, table), (thin_hbm, thin), (off_hbm, off_ref)))
    ]
    for copy in extra:
        copy.start()
    greet(count, at)
    arrive = start_shear(shear, xbuf, asend, arecv, loc.at[pl.ds(3, 2)])
    for copy in extra:
        copy.wait()
    full, part = 2 * LANES, LANES
    starts = [i * full for i in range(8)] + [8 * full + i * part for i in range(4)]
    sizes_of = [full] * 8 + [part] * 4
    t = [table.at[a : a + n] for a, n in zip(starts, sizes_of)]
    h = nx // LANES // 2
    tc, ts, tw = thin.at[0:h], thin.at[h : 2 * h], thin.at[2 * h : 2 * h + LANES]
    leave = forward_y(arrive, xbuf, ((t[0], t[1]), (t[2], t[3])), tc, ts, spec, sbuf, bsend, brecv, loc.at[pl.ds(5, 2)])
    middle(nx, leave, gbuf, wbuf, spec, smooth_ref, (t[8], t[9]), (t[10], t[11]), tw, zbuf, field, csend, crecv, loc.at[pl.ds(7, 1)])
    inverse_y(zbuf, ((t[4], t[5]), (t[6], t[7])), tc, ts, x_ref, sq_ref, top_ref, bot_ref)
    peaks(float(nx * ny), x_ref, sq_ref, top_ref, bot_ref, off_ref, thr_ref, rms_ref, high_ref, cnt_ref,
          cnt_own, wide, above_ref, below_ref, slots, esend, erecv, hsend, hrecv)


VM = pl.BlockSpec(memory_space=pltpu.VMEM)
HB = pl.BlockSpec(memory_space=pltpu.HBM)
SM = pl.BlockSpec(memory_space=pltpu.SMEM)
F32 = jnp.float32


def shape(*dims):
    return jax.ShapeDtypeStruct(dims, F32)


def one_map(shear, smoothing, offsets, thresholds):
    rows_in, cols_in = shear.shape[1:]
    nrow, ncol = lax.axis_size("row"), lax.axis_size("col")
    nx, ny = rows_in * nrow, cols_in * ncol
    count = nrow * ncol
    rows = nx // count
    base, first, inv, first_inv, tc, ts = y_tables(ny)
    fwd_x, inv_x, tw_x = x_tables(nx)
    parts = [half for t in (base, first, inv, first_inv, fwd_x, inv_x) for half in split_table(t)]
    table = jnp.concatenate(parts, axis=0)
    tw_x = np.pad(tw_x, ((0, 0), (0, LANES - tw_x.shape[1])))
    thin = jnp.asarray(np.concatenate([tc, ts, tw_x], axis=0).astype(np.float32))
    dma = pltpu.SemaphoreType.DMA
    vm = lambda *dims: pltpu.VMEM(dims, F32)
    kappa, rms, heights, counts = pl.pallas_call(
        partial(kernel, (nx, ny)),
        out_shape=(shape(rows, ny), shape(1, LANES), shape(*offsets.shape), shape(1, LANES)),
        in_specs=[HB, SM, HB, SM, HB, HB],
        out_specs=(VM, VM, VM, VM),
        scratch_shapes=[
            vm(2, ncol, rows, cols_in),
            vm(count, 2, rows, LANES),
            vm(count, 2, rows, LANES),
            vm(nx // LANES, LANES, LANES),
            vm(nx // LANES + 1, 2, LANES, LANES),
            vm(count, rows, LANES),
            vm(count, rows, LANES),
            vm(rows + 16, ny),
            pltpu.VMEM(offsets.shape, jnp.int32),
            pltpu.VMEM(table.shape, jnp.bfloat16),
            vm(*thin.shape),
            vm(1, LANES), vm(1, LANES),
            vm(1, ny), vm(1, ny), vm(1, ny), vm(1, ny),
            vm(2, count - 1, 1, LANES),
            dma((2, ncol)), dma((2, ncol)), dma((2, count)), dma((2, count)), dma((count,)), dma((count,)),
            dma((2, count - 1)), dma((2, count - 1)), dma((2,)), dma((2,)), dma((8,)),
        ],
        compiler_params=pltpu.CompilerParams(
            vmem_limit_bytes=63 * 2**20, collective_id=0, has_side_effects=True
        ),
    )(shear, smoothing, offsets, thresholds, table, thin)
    return kappa / rms[:, :1], heights, counts[0, : thresholds.shape[0]]


def body(shear, smoothing, offsets, thresholds):
    outs = [
        one_map(shear[:, m], smoothing[m : m + 1], offsets[m], thresholds[m])
        for m in range(shear.shape[1])
    ]
    return tuple(jnp.stack(parts) for parts in zip(*outs))


def solution(mesh):
    return jax.shard_map(
        body,
        mesh=mesh,
        in_specs=(
            P(None, "maps", "row", "col"),
            P("maps"),
            P("maps", GROUP, None),
            P("maps", None),
        ),
        out_specs=(P("maps", GROUP, None), P("maps", GROUP, None), P("maps", None)),
        check_vma=False,
    )
```
